32 devices in a mesh: groups: 2 (over x), ep: 16 (over z, y, core).
Axes of the slice: x: 2, y: 2, z: 4, core: 2. Of those that a mesh axis runs over, the one named last changes fastest.
Arguments:
- states: float32 [2, 256, 2048], P(None, ('groups', 'ep')), parts along dimension 1, may hold values from -6 to 6
- attn_gain: float32 [2048], replicated, may hold values from 0.1 to 1.9
- moe_gain: float32 [2048], replicated, may hold values from 0.1 to 1.9
- w_query: bfloat16 [2048, 2048], P(None, 'ep'), may hold values from -11 to 11
- w_key: bfloat16 [2048, 256], P(None, 'ep'), may hold values from -0.125 to 0.125
- w_value: bfloat16 [2048, 256], P(None, 'ep'), may hold values from -0.125 to 0.125
- w_output: bfloat16 [2048, 2048], P('ep'), may hold values from -0.125 to 0.125
- w_gate_up: bfloat16 [16, 2048, 1536], P('ep'), may hold values from -0.125 to 0.125
- w_down: bfloat16 [16, 768, 2048], P('ep'), may hold values from -0.21875 to 0.21875
- key_cache: bfloat16 [64, 1024, 256], P(('groups', 'ep')), parts along dimension 0, may hold values from -60 to 60
- value_cache: bfloat16 [64, 1024, 256], P(('groups', 'ep')), parts along dimension 0, may hold values from -24 to 24
- cache_lengths: int32 [64], P(('groups', 'ep')), parts along dimension 0, may hold values from 1 to 1024, as said below
- prefix_slot: int32 [256], P(('groups', 'ep')), parts along dimension 0, may hold values from 0 to 1
- routes: int32 [256, 2, 8], P(('groups', 'ep')), parts along dimension 0, may hold values from 0 to 15, all different within a row; in each aligned block of 16 rows (0 to 15, 16 to 31, ..., all dimensions but the last counted through in order) at most 16 rows name the same one
- gate_weights: float32 [2, 256, 8], P(None, ('groups', 'ep')), parts along dimension 1, may hold values from 0.05 to 0.5
Outputs:
- layer_out: float32 [2, 256, 2048], P(None, ('groups', 'ep')), parts along dimension 1
- appended_kv: bfloat16 [2, 256, 512], P(None, ('groups', 'ep')), parts along dimension 1
The draws below stay inside these ranges and needn't reach their ends.
There are 2 independent parts, one for each index of `groups`. The reference program is written for one: setup_inputs(seed, part) draws one part's arguments, and reference() takes and returns one part's arrays. A program takes and returns all parts, laid end to end along the dimension named above; an argument that names none is the same for every part. Nothing has to cross between parts.
Inputs may be any that keep to these rules, and one draw needn't show every extreme that they name: `cache_lengths`: positions beyond a prefix's length are unused; some prefix is full at 1024. `routes`: over both steps together, the 8 branches of one ep device choose any one expert at most 16 times; a branch's 8 experts at one step differ.
All inputs are finite; a program needn't handle non-finite values.
Results may differ from the reference program's by a relative error of at most 0.0024.
The reference program's roundings to bfloat16 on the way count: a program that leaves them out, or rounds other values in their place, can miss the bound.
Values may be sent and summed in bfloat16 or wider, within the bound.
A program may use at most 128 MiB of HBM per device.

```python
import math
import jax
import jax.numpy as jnp
import numpy as np
from jax import lax

D = 2048
HQ = 16
KVH = 2
HD = 128
FF = 768
TOPK = 8
BR_DEV = 8
PREF_DEV = 2
CACHE = 1024
EXPERTS = 16
B = 128
PREFIXES = 32
CAP = 16
N_EP = 16


def draw_cache_lengths(key, part):
    lengths = jax.random.randint(key, (PREFIXES,), 1, CACHE + 1, dtype=jnp.int32)
    return lengths.at[0].set(CACHE)


def draw_w_query(key, part):
    base = jax.random.truncated_normal(key, -6.0, 6.0, (D, HQ * HD), jnp.float32) * D ** (-0.5)
    return base.astype(jnp.bfloat16)


def draw_key_cache(key, part):
    base = jax.random.truncated_normal(key, -6.0, 6.0, (PREFIXES, CACHE, KVH * HD), jnp.float32) * 1.5
    return base.astype(jnp.bfloat16)


def set_ends(drawn, own_key, least, high):
    longest = drawn.shape.index(max(drawn.shape))
    spots = []
    for shift in (0, 1):
        where = [jax.random.randint(jax.random.fold_in(own_key, axis), (), 0, length) for axis, length in enumerate(drawn.shape)]
        where[longest] = (where[longest] + shift) % drawn.shape[longest]
        spots.append(tuple(where))
    return drawn.at[spots[0]].set(least).at[spots[1]].set(high)


def block_levels(key, shape, cuts, low, high):
    factor_of, own = 1.0, jax.random.fold_in(key, 6)
    for axis_at, shards_of in cuts:
        heights = jnp.exp(jax.random.uniform(jax.random.fold_in(own, axis_at), (shards_of,), jnp.float32, low / len(cuts), high / len(cuts)))
        factor_of = factor_of * jnp.repeat(heights, shape[axis_at] // shards_of).reshape([-1 if axis == axis_at else 1 for axis in range(len(shape))])
    return factor_of


def assign_block(own_key, own, number, rows, number_of, top, most, slope):
    ranking = jax.random.permutation(own_key, number_of)
    heavy_load, ordinary = portions_of(number_of, rows * top, most, slope, True), portions_of(number_of, rows * top, most, slope, False)
    places = jnp.arange(number_of)

    def named(sizes, offset_by):
        used = int((sizes > 0).sum())
        fixed = max(1, used // 4)
        passed = fixed + (places - fixed + offset_by * (used - fixed)) % max(1, number_of - fixed)
        return jnp.zeros((number_of,), jnp.int32).at[ranking[jnp.where(places < fixed, places, passed)]].set(jnp.asarray(sizes, jnp.int32))

    sizes = jnp.where(number % 4 == 0, named(heavy_load, number // 4), named(ordinary, number - number // 4 - 1))
    mixed = jax.random.permutation(jax.random.fold_in(own, 3), number_of)
    giver, receiver = mixed[0:number_of // 2 * 2:2], mixed[1:number_of // 2 * 2:2]
    margin = jnp.minimum(sizes[giver] - 1, most - sizes[receiver]) // 2
    margin = jnp.where((giver == ranking[0]) | (receiver == ranking[0]) | (sizes[receiver] == 0), 0, jnp.maximum(margin, 0))
    passed = jax.random.randint(jax.random.fold_in(own, 4), (number_of // 2,), 0, 1 << 20) % (margin + 1)
    sizes = sizes.at[giver].add(-passed).at[receiver].add(passed)
    items = jnp.searchsorted(jnp.cumsum(sizes), jnp.arange(rows * top), side="right").astype(jnp.int32)
    listing = items.reshape(top, rows).T
    listing = listing[jax.random.permutation(jax.random.fold_in(own, 1), rows)]
    offset_by = jax.random.randint(jax.random.fold_in(own, 2), (rows, 1), 0, top)
    return jnp.take_along_axis(listing, (jnp.arange(top)[None, :] + offset_by) % top, axis=1)


def portions_of(amount, total, bound, slope, full):
    weights = [(1 << 20) // math.isqrt(rank ** slope) + 1 for rank in range(1, amount + 1)]
    largest = bound if full else min(bound, max(-(-total // amount), total * weights[0] // sum(weights)))
    least = 1 if total - largest >= amount - 1 else 0
    given, surplus = [largest] + [least] * (amount - 1), total - largest - least * (amount - 1)
    while surplus > 0:
        movable = [i for i in range(1, amount) if given[i] < largest] or [i for i in range(1, amount) if given[i] < bound]
        mass, left = sum([weights[i] for i in movable]), surplus
        for i in movable:
            addition = min(bound - given[i], max(1, left * weights[i] // mass), surplus)
            given[i] = given[i] + addition
            surplus = surplus - addition
    return np.array(given)


def scatter_about(own_key, dims, width, limit, cuts=(), kind=jnp.bfloat16):
    values = width * jax.random.normal(own_key, dims, jnp.float32)
    if cuts:
        values = values * block_levels(own_key, dims, cuts, -0.22, 0.18)
    return jnp.clip(values, -limit, limit).astype(kind)


def setup_inputs(seed: int = 0, part: int = 0) -> dict:
    key_list = jax.random.split(jax.random.key(seed), 16)
    own_keys = jax.random.split(jax.random.fold_in(key_list[15], part), 16)
    states = scatter_about(own_keys[0], (2, B, D), 1.0, 6.0, ((1, 16),), jnp.float32)
    attn_gain = jnp.clip(1.0 + 0.18 * jax.random.normal(key_list[1], (D,), jnp.float32), 0.1, 1.9)
    moe_gain = jnp.clip(1.0 + 0.18 * jax.random.normal(key_list[2], (D,), jnp.float32), 0.1, 1.9)
    w_query = draw_w_query(jax.random.fold_in(key_list[15], 71), part)
    w_key = scatter_about(key_list[4], (D, KVH * HD), D ** -0.5, 0.125, ((1, 16),))
    w_value = scatter_about(key_list[5], (D, KVH * HD), D ** -0.5, 0.125, ((1, 16),))
    w_output = scatter_about(key_list[6], (HQ * HD, D), (HQ * HD) ** -0.5, 0.125, ((0, 16),))
    w_gate_up = scatter_about(key_list[7], (EXPERTS, D, 2 * FF), D ** -0.5, 0.125, ((0, 16),))
    w_down = scatter_about(key_list[8], (EXPERTS, FF, D), FF ** -0.5, 0.21875, ((0, 16),))
    key_cache = draw_key_cache(jax.random.fold_in(jax.random.fold_in(key_list[15], part), 71), part)
    value_cache = scatter_about(own_keys[10], (PREFIXES, CACHE, KVH * HD), 4.0, 24.0, ((0, 16),))
    cache_lengths = draw_cache_lengths(jax.random.fold_in(jax.random.fold_in(key_list[15], part), 71), part)
    prefix_slot = set_ends(jax.random.randint(own_keys[12], (B,), 0, PREF_DEV), jax.random.fold_in(own_keys[12], 1), 0, PREF_DEV - 1).astype(jnp.int32)
    routes_keys = jax.random.split(jax.random.fold_in(own_keys[13], 1), B * 2 // (2 * BR_DEV))
    routes_turns = jax.random.permutation(jax.random.fold_in(own_keys[13], 3), B * 2 // (2 * BR_DEV))
    routes = jax.vmap(lambda own, number: assign_block(jax.random.fold_in(own_keys[13], 2), own, number, 2 * BR_DEV, EXPERTS, TOPK, CAP, 2))(routes_keys, routes_turns).reshape((B, 2, TOPK))
    gate_weights = jnp.clip(jnp.exp(math.log(0.5) - 2.3025851 * jax.random.uniform(own_keys[14], (2, B, TOPK), jnp.float32) ** block_levels(own_keys[14], (2, B, TOPK), ((1, 16),), -0.2, 0.2)), 0.05, 0.5)
    return {"states": states, "attn_gain": attn_gain, "moe_gain": moe_gain, "w_query": w_query, "w_key": w_key, "w_value": w_value, "w_output": w_output, "w_gate_up": w_gate_up, "w_down": w_down, "key_cache": key_cache, "value_cache": value_cache, "cache_lengths": cache_lengths, "prefix_slot": prefix_slot, "routes": routes, "gate_weights": gate_weights}


EPS = 1e-06
THETA = 1000000.0

def rms_scale(values, gain):
    squares = lax.optimization_barrier(jnp.mean(values * values, axis=-1, keepdims=True))
    return values * lax.rsqrt(squares + EPS) * gain

def rotate(vectors, positions):
    head_size = vectors.shape[-1]
    half_size = head_size // 2
    inverse_rate = THETA ** (-(jnp.arange(half_size).astype(jnp.float32) * 2.0 / head_size))
    phases = positions[..., None, None] * inverse_rate
    cosine = jnp.cos(phases)
    sine_part = jnp.sin(phases)
    first_half = vectors[..., :half_size]
    second_half = vectors[..., half_size:]
    return jnp.concatenate([first_half * cosine - second_half * sine_part, second_half * cosine + first_half * sine_part], axis=-1)

def attend_block(packed):
    queries, new_keys, new_values, key_block, value_block, lengths, slots = packed
    step_count, row_count, head_count, head_size = queries.shape
    prefix_count, cache_span, kv_heads, _ = key_block.shape
    group_size = head_count // kv_heads
    grouped = queries.reshape(step_count, row_count, kv_heads, group_size, head_size).astype(jnp.float32)
    inv_root = 1.0 / math.sqrt(head_size)
    far_scores = jnp.einsum('srkgd,pckd->srkgpc', grouped, key_block.astype(jnp.float32)) * inv_root
    visible = (jnp.arange(cache_span)[None, None, :] < lengths[None, :, None]) & (slots[:, None, None] == jnp.arange(prefix_count)[None, :, None])
    far_scores = jnp.where(visible[None, :, None, None], far_scores, -1e+30)
    own_scores = jnp.einsum('srkgd,trkd->srkgt', grouped, new_keys.astype(jnp.float32)) * inv_root
    causal = jnp.arange(step_count)[None, :] <= jnp.arange(step_count)[:, None]
    own_scores = jnp.where(causal[:, None, None, None, :], own_scores, -1e+30)
    peak = jnp.maximum(lax.optimization_barrier(jnp.max(far_scores, axis=(-2, -1))), lax.optimization_barrier(jnp.max(own_scores, axis=-1)))
    far_weights = jnp.exp(far_scores - peak[..., None, None])
    own_weights = jnp.exp(own_scores - peak[..., None])
    normalizer = lax.optimization_barrier(jnp.sum(far_weights, axis=(-2, -1))) + lax.optimization_barrier(jnp.sum(own_weights, axis=-1))
    far_probs = (far_weights / normalizer[..., None, None]).astype(jnp.bfloat16)
    own_probs = (own_weights / normalizer[..., None]).astype(jnp.bfloat16)
    attended = jnp.einsum('srkgpc,pckd->srkgd', far_probs.astype(jnp.float32), value_block.astype(jnp.float32))
    attended = attended + jnp.einsum('srkgt,trkd->srkgd', own_probs.astype(jnp.float32), new_values.astype(jnp.float32))
    return attended.reshape(step_count, row_count, head_count * head_size).astype(jnp.bfloat16)

def reference(states, attn_gain, moe_gain, w_query, w_key, w_value, w_output, w_gate_up, w_down, key_cache, value_cache, cache_lengths, prefix_slot, routes, gate_weights):
    normed = rms_scale(states, attn_gain).astype(jnp.bfloat16)
    flat_normed = normed.reshape(2 * B, D).astype(jnp.float32)
    queries = jnp.dot(flat_normed, w_query.astype(jnp.float32)).reshape(2, B, HQ, HD)
    new_keys = jnp.dot(flat_normed, w_key.astype(jnp.float32)).reshape(2, B, KVH, HD)
    new_values = jnp.dot(flat_normed, w_value.astype(jnp.float32)).reshape(2, B, KVH, HD).astype(jnp.bfloat16)
    prefix_id = (jnp.arange(B) // BR_DEV * PREF_DEV + prefix_slot).astype(jnp.int32)
    positions = cache_lengths[prefix_id].astype(jnp.float32)[None, :] + jnp.arange(2).astype(jnp.float32)[:, None]
    queries = rotate(queries, positions).astype(jnp.bfloat16)
    new_keys = rotate(new_keys, positions).astype(jnp.bfloat16)

    def by_block(array):
        return jnp.swapaxes(array.reshape((2, N_EP, BR_DEV) + array.shape[2:]), 0, 1)
    attended = lax.map(attend_block, (by_block(queries), by_block(new_keys), by_block(new_values), key_cache.reshape(N_EP, PREF_DEV, CACHE, KVH, HD), value_cache.reshape(N_EP, PREF_DEV, CACHE, KVH, HD), cache_lengths.reshape(N_EP, PREF_DEV), prefix_slot.reshape(N_EP, BR_DEV)))
    attended = jnp.swapaxes(attended, 0, 1).reshape(2 * B, HQ * HD)
    projected = jnp.dot(attended.astype(jnp.float32), w_output.astype(jnp.float32)).reshape(2, B, D)
    hidden = states + projected
    moe_input = rms_scale(hidden, moe_gain).astype(jnp.bfloat16).reshape(2 * B, D)
    flat_routes = jnp.swapaxes(routes, 0, 1).reshape(-1).astype(jnp.int32)
    total_count = flat_routes.shape[0]
    sorted_ids = jnp.argsort(flat_routes, stable=True).astype(jnp.int32)
    counts = lax.optimization_barrier(jnp.sum((flat_routes[:, None] == jnp.arange(EXPERTS)[None, :]).astype(jnp.int32), axis=0))
    starts = (jnp.cumsum(counts) - counts).astype(jnp.int32)
    row_limit = N_EP * CAP
    padded_ids = jnp.concatenate([sorted_ids, jnp.zeros((row_limit,), jnp.int32)])

    def run_expert(expert_id):
        chosen = lax.dynamic_slice_in_dim(padded_ids, starts[expert_id], row_limit)
        inputs = moe_input[chosen // TOPK].astype(jnp.float32)
        both = jnp.dot(inputs, w_gate_up[expert_id].astype(jnp.float32))
        activation = (jax.nn.silu(both[:, :FF]) * both[:, FF:]).astype(jnp.bfloat16)
        return jnp.dot(activation.astype(jnp.float32), w_down[expert_id].astype(jnp.float32)).astype(jnp.bfloat16)
    outputs = lax.map(run_expert, jnp.arange(EXPERTS).astype(jnp.int32))
    within = jnp.zeros((total_count,), jnp.int32).at[sorted_ids].set(jnp.arange(total_count).astype(jnp.int32) - starts[flat_routes[sorted_ids]])
    picked = outputs[flat_routes, within].astype(jnp.float32).reshape(2, B, TOPK, D)
    mixture = lax.optimization_barrier(jnp.sum(gate_weights[..., None] * picked, axis=2))
    appended = jnp.concatenate([new_keys.reshape(2, B, KVH * HD), new_values.reshape(2, B, KVH * HD)], axis=-1)
    return (hidden + mixture, appended)
```

```python
import math

import jax
import jax.numpy as jnp
from jax import lax
from jax.experimental import pallas as pl
from jax.experimental.pallas import tpu as pltpu
from jax.sharding import PartitionSpec as P

HQ = 16
KVH = 2
HD = 128
TOPK = 8


EPS = 1e-06
THETA = 1000000.0


def rms_scale(values, gain):
    squares = jnp.mean(values * values, axis=-1, keepdims=True)
    return values * lax.rsqrt(squares + EPS) * gain


def rotate(vectors, positions):
    head_size = vectors.shape[-1]
    half_size = head_size // 2
    inverse_rate = THETA ** (-(jnp.arange(half_size).astype(jnp.float32) * 2.0 / head_size))
    phases = positions[..., None, None] * inverse_rate
    cosine = jnp.cos(phases)
    sine_part = jnp.sin(phases)
    first_half = vectors[..., :half_size]
    second_half = vectors[..., half_size:]
    return jnp.concatenate(
        [
            first_half * cosine - second_half * sine_part,
            second_half * cosine + first_half * sine_part,
        ],
        axis=-1,
    )


def attend_block(queries, new_keys, new_values, key_block, value_block, lengths, slots):
    step_count, row_count, head_count, head_size = queries.shape
    prefix_count, cache_span, kv_heads, _ = key_block.shape
    group_size = head_count // kv_heads
    grouped = queries.reshape(step_count, row_count, kv_heads, group_size, head_size)
    inv_root = 1.0 / math.sqrt(head_size)
    far_scores = (
        jnp.einsum("srkgd,pckd->srkgpc", grouped, key_block, preferred_element_type=jnp.float32)
        * inv_root
    )
    visible = (jnp.arange(cache_span)[None, None, :] < lengths[None, :, None]) & (
        slots[:, None, None] == jnp.arange(prefix_count)[None, :, None]
    )
    far_scores = jnp.where(visible[None, :, None, None], far_scores, -1e30)
    own_scores = (
        jnp.einsum("srkgd,trkd->srkgt", grouped, new_keys, preferred_element_type=jnp.float32)
        * inv_root
    )
    causal = jnp.arange(step_count)[None, :] <= jnp.arange(step_count)[:, None]
    own_scores = jnp.where(causal[:, None, None, None, :], own_scores, -1e30)
    peak = jnp.maximum(jnp.max(far_scores, axis=(-2, -1)), jnp.max(own_scores, axis=-1))
    far_weights = jnp.exp(far_scores - peak[..., None, None])
    own_weights = jnp.exp(own_scores - peak[..., None])
    normalizer = jnp.sum(far_weights, axis=(-2, -1)) + jnp.sum(own_weights, axis=-1)
    far_probs = (far_weights / normalizer[..., None, None]).astype(jnp.bfloat16)
    own_probs = (own_weights / normalizer[..., None]).astype(jnp.bfloat16)
    attended = jnp.einsum(
        "srkgpc,pckd->srkgd", far_probs, value_block, preferred_element_type=jnp.float32
    )
    attended = attended + jnp.einsum(
        "srkgt,trkd->srkgd", own_probs, new_values, preferred_element_type=jnp.float32
    )
    return attended.reshape(step_count, row_count, head_count * head_size).astype(jnp.bfloat16)


def shards(
    states,
    attn_gain,
    moe_gain,
    w_query,
    w_key,
    w_value,
    w_output,
    w_gate_up,
    w_down,
    key_cache,
    value_cache,
    cache_lengths,
    prefix_slot,
    routes,
    gate_weights,
):
    devices = lax.axis_size("ep")
    step_count, row_count, model_width = states.shape
    query_cols = w_query.shape[1]
    kv_cols = w_key.shape[1]
    normed = rms_scale(states, attn_gain).astype(jnp.bfloat16)
    joined = jnp.concatenate([w_query, w_key, w_value], axis=1)
    head_parts = jnp.einsum(
        "srd,dc->src",
        lax.all_gather(normed, "ep", axis=1, tiled=True),
        joined,
        preferred_element_type=jnp.float32,
    )
    own_cols = lax.all_to_all(head_parts, "ep", split_axis=1, concat_axis=2, tiled=True)
    own_cols = own_cols.reshape(step_count, row_count, devices, query_cols + 2 * kv_cols)
    queries = own_cols[..., :query_cols].reshape(step_count, row_count, HQ, HD)
    new_keys = own_cols[..., query_cols : query_cols + kv_cols].reshape(
        step_count, row_count, KVH, HD
    )
    new_values = (
        own_cols[..., query_cols + kv_cols :]
        .reshape(step_count, row_count, KVH, HD)
        .astype(jnp.bfloat16)
    )
    prefix_count, cache_span, _ = key_cache.shape
    lengths_here = jnp.sum(
        jnp.where(
            prefix_slot[:, None] == jnp.arange(prefix_count)[None, :], cache_lengths[None, :], 0
        ),
        axis=1,
    )
    positions = (
        lengths_here.astype(jnp.float32)[None, :]
        + jnp.arange(step_count).astype(jnp.float32)[:, None]
    )
    queries = rotate(queries, positions).astype(jnp.bfloat16)
    new_keys = rotate(new_keys, positions).astype(jnp.bfloat16)
    attended = attend_block(
        queries,
        new_keys,
        new_values,
        key_cache.reshape(prefix_count, cache_span, KVH, HD),
        value_cache.reshape(prefix_count, cache_span, KVH, HD),
        cache_lengths,
        prefix_slot,
    )
    w_columns = lax.all_to_all(w_output, "ep", split_axis=1, concat_axis=0, tiled=True)
    column_part = jnp.einsum(
        "srf,fc->src",
        lax.all_gather(attended, "ep", axis=1, tiled=True),
        w_columns,
        preferred_element_type=jnp.float32,
    )
    projected = lax.all_to_all(column_part, "ep", split_axis=1, concat_axis=2, tiled=True)
    hidden = states + projected
    moe_input = (
        rms_scale(hidden, moe_gain)
        .astype(jnp.bfloat16)
        .reshape(step_count * row_count, model_width)
    )
    expert_count = w_gate_up.shape[0] * devices
    capacity = max(2, 4 * row_count * TOPK // expert_count)
    flat_routes = jnp.swapaxes(routes, 0, 1).reshape(-1)
    onehot = (flat_routes[:, None] == jnp.arange(expert_count)[None, :]).astype(jnp.int32)
    running = jnp.cumsum(onehot, axis=0) - 1
    within = jnp.sum(onehot * running, axis=1)
    slot_index = flat_routes * capacity + within
    dispatch = (jnp.arange(expert_count * capacity)[:, None] == slot_index[None, :]).astype(
        jnp.bfloat16
    )
    repeated = jnp.repeat(moe_input, TOPK, axis=0)
    outgoing = jnp.dot(dispatch, repeated, preferred_element_type=jnp.float32).astype(jnp.bfloat16)
    outgoing = outgoing.reshape(expert_count, capacity, model_width)
    both = jnp.einsum(
        "nsd,df->nsf",
        lax.all_to_all(outgoing, "ep", split_axis=0, concat_axis=0, tiled=True),
        w_gate_up[0],
        preferred_element_type=jnp.float32,
    )
    half_cols = both.shape[-1] // 2
    activation = (jax.nn.silu(both[..., :half_cols]) * both[..., half_cols:]).astype(jnp.bfloat16)
    expert_done = jnp.einsum(
        "nsf,fd->nsd", activation, w_down[0], preferred_element_type=jnp.float32
    ).astype(jnp.bfloat16)
    returned = lax.all_to_all(expert_done, "ep", split_axis=0, concat_axis=0, tiled=True)
    picked = returned.reshape(expert_count * capacity, model_width)[slot_index]
    picked = picked.astype(jnp.float32).reshape(step_count, row_count, TOPK, model_width)
    mixture = jnp.sum(gate_weights[..., None] * picked, axis=2)
    appended = jnp.concatenate(
        [
            new_keys.reshape(step_count, row_count, KVH * HD),
            new_values.reshape(step_count, row_count, KVH * HD),
        ],
        axis=-1,
    )
    return (hidden + mixture, appended)


TUNED_DEVICES = 16
ROWS = 16


def norm_rows(values, gain):
    squares = jnp.mean(values * values, axis=-1, keepdims=True)
    return values * lax.rsqrt(squares + EPS) * gain


def layer_kernel(
    states,
    attn_gain,
    moe_gain,
    w_query,
    w_key,
    w_value,
    aux,
    gates,
    w_output,
    w_gate_up,
    w_down,
    key_cache,
    value_cache,
    out,
    appended,
    w_joined,
    gather_q,
    gather_o,
    gather_m,
    parts,
    own_parts,
    w_cols,
    cols,
    own_cols,
    hidden,
    act,
    expert_out,
    returned,
    fresh_k,
    fresh_v,
    queries,
    gate_up_v,
    down_v,
    keys_v,
    values_v,
    load_sem,
    ag_send,
    ag_recv,
    a2a_send,
    a2a_recv,
):
    n = TUNED_DEVICES
    half = n // 2
    me = lax.axis_index("ep")
    c = me % 2
    y = (me // 2) % 2
    z = me // 4
    near = me // half
    z_other = (z, z + 1 - 2 * (z % 2), (z + 2) % 4, 3 - z)

    def index_of(zz, yy, cc):
        return (zz * 2 + yy) * 2 + cc

    def block(ref, i, rows=ROWS):
        return ref.at[pl.ds(pl.multiple_of(i * rows, rows), rows), :]

    def rdma(src, dst, send, recv, target):
        return pltpu.make_async_remote_copy(
            src_ref=src,
            dst_ref=dst,
            send_sem=send,
            recv_sem=recv,
            device_id={"ep": target},
            device_id_type=pl.DeviceIdType.MESH,
        )

    barrier = pltpu.get_barrier_semaphore()
    for i in range(1, n):
        pl.semaphore_signal(
            barrier,
            inc=1,
            device_id={"ep": (me + i) % n},
            device_id_type=pl.DeviceIdType.MESH,
        )

    loads = [
        pltpu.make_async_copy(key_cache, keys_v, load_sem.at[0]),
        pltpu.make_async_copy(value_cache, values_v, load_sem.at[1]),
        pltpu.make_async_copy(w_gate_up, gate_up_v, load_sem.at[2]),
        pltpu.make_async_copy(w_down, down_v, load_sem.at[3]),
        pltpu.make_async_copy(
            w_output.at[:, pl.ds(pl.multiple_of(me * 128, 128), 128)],
            block(w_cols, me, 128),
            load_sem.at[4],
        ),
    ]
    for load in loads:
        load.start()

    class Gather:
        def __init__(self, buf, phase):
            self.buf, self.phase, self.sends = buf, phase, []

        def push(self, src, target):
            k = len(self.sends)
            copy = rdma(
                block(self.buf, src),
                block(self.buf, src),
                ag_send.at[self.phase, k],
                ag_recv.at[self.phase, src],
                target,
            )
            copy.start()
            self.sends.append(copy)

        def arrived(self, src):
            rdma(
                block(self.buf, src),
                block(self.buf, src),
                ag_send.at[self.phase, 0],
                ag_recv.at[self.phase, src],
                index_of(z, y, 1 - c),
            ).wait_recv()

        def begin(self):
            for i in (2, 3, 1):
                self.push(me, index_of(z_other[i], y, c))
            self.push(me, index_of(z, 1 - y, c))
            self.push(me, index_of(z, y, 1 - c))

        def from_z(self, i):
            src = index_of(z_other[i], y, c)
            self.arrived(src)
            self.push(src, index_of(z, 1 - y, c))
            self.push(src, index_of(z, y, 1 - c))

        def from_y(self, i):
            src = index_of(z_other[i], 1 - y, c)
            self.arrived(src)
            self.push(src, index_of(z, y, 1 - c))

        def from_core(self, i):
            self.arrived(index_of(z_other[i], y, 1 - c))
            self.arrived(index_of(z_other[i], 1 - y, 1 - c))

        def near_ready(self):
            self.from_y(0)
            self.from_z(1)
            self.from_y(1)
            self.from_core(0)
            self.from_core(1)

        def far_forward(self):
            self.from_z(2)
            self.from_z(3)

        def far_ready(self):
            self.from_y(2)
            self.from_y(3)
            self.from_core(2)
            self.from_core(3)

        def finish(self):
            for copy in self.sends:
                copy.wait_send()

    def scatter(src, dst, phase, group, is_near):
        first = 1 if is_near else 0
        for i in range(first, half):
            p = group * half + (me + i) % half
            rdma(
                block(src, p),
                block(dst, me),
                a2a_send.at[phase, p],
                a2a_recv.at[phase, me],
                p,
            ).start()
        if is_near:
            block(dst, me)[...] = block(src, me)[...]

    def scatter_wait(src, dst, phase, rows=ROWS):
        for i in range(1, n):
            p = (me + i) % n
            rdma(
                block(src, p, rows),
                block(dst, p, rows),
                a2a_send.at[phase, p],
                a2a_recv.at[phase, p],
                p,
            ).wait_recv()

    def scatter_sent(src, dst, phase):
        for i in range(1, n):
            p = (me + i) % n
            rdma(
                block(src, p),
                block(dst, p),
                a2a_send.at[phase, p],
                a2a_recv.at[phase, p],
                p,
            ).wait_send()

    def w_copy(p, landing):
        return rdma(
            w_output.at[:, pl.ds(pl.multiple_of(p * 128, 128), 128)],
            block(w_cols, landing, 128),
            a2a_send.at[3, p],
            a2a_recv.at[3, landing],
            p,
        )

    block(gather_q, me)[...] = norm_rows(states[...], attn_gain[...]).astype(jnp.bfloat16)
    pl.semaphore_wait(barrier, n - 1)

    first = Gather(gather_q, 0)
    first.begin()
    w_joined[:, 0:128] = w_query[...]
    w_joined[:, 128:144] = w_key[...]
    w_joined[:, 144:160] = w_value[...]
    w_joined[:, 160:256] = jnp.zeros((w_joined.shape[0], 96), jnp.bfloat16)

    def group_rows(group):
        return pl.ds(pl.multiple_of(group * 128, 128), 128)

    first.near_ready()
    parts[group_rows(near), :] = jnp.dot(
        gather_q[group_rows(near), :], w_joined[...], preferred_element_type=jnp.float32
    )
    scatter(parts, own_parts, 0, near, True)
    first.far_forward()
    first.far_ready()
    parts[group_rows(1 - near), :] = jnp.dot(
        gather_q[group_rows(1 - near), :], w_joined[...], preferred_element_type=jnp.float32
    )
    scatter(parts, own_parts, 0, 1 - near, False)
    for i in range(1, n):
        w_copy((me + i) % n, me).start()
    first.finish()
    scatter_wait(parts, own_parts, 0)

    cosine = aux[:, 0:128]
    sine = aux[:, 128:256]

    def turned(vectors):
        return vectors * cosine + pltpu.roll(vectors, 64, 1) * sine

    for j in range(n):
        rows = slice(j * ROWS, (j + 1) * ROWS)
        queries[rows, :] = turned(own_parts[rows, 0:128]).astype(jnp.bfloat16)
        fresh_k[:, j * 16 : (j + 1) * 16] = own_parts[rows, 128:144]
        fresh_v[:, j * 16 : (j + 1) * 16] = own_parts[rows, 144:160]
    loads[0].wait()
    loads[1].wait()
    inv_root = 1.0 / math.sqrt(HD)
    group_size = HQ // KVH
    q_rows = group_size * ROWS
    span = keys_v.shape[1]
    far_pos = lax.broadcasted_iota(jnp.int32, (q_rows, span), 1).astype(jnp.float32)
    row_at = lax.broadcasted_iota(jnp.int32, (q_rows, ROWS), 0) % ROWS
    col_at = lax.broadcasted_iota(jnp.int32, (q_rows, ROWS), 1)
    own_seen = (row_at % 8 == col_at % 8) & (col_at // 8 <= row_at // 8)
    limits = [jnp.concatenate([aux[:, 256 + p : 257 + p]] * group_size, axis=0) for p in range(2)]
    for k in range(KVH):
        lanes = slice(k * HD, (k + 1) * HD)
        new_keys = turned(fresh_k[:, lanes]).astype(jnp.bfloat16)
        new_values = fresh_v[:, lanes].astype(jnp.bfloat16)
        appended[:, lanes] = new_keys
        appended[:, slice((KVH + k) * HD, (KVH + k + 1) * HD)] = new_values
        q = queries[k * q_rows : (k + 1) * q_rows, :]

        def against(rows):
            return (
                lax.dot_general(
                    q, rows, (((1,), (1,)), ((), ())), preferred_element_type=jnp.float32
                )
                * inv_root
            )

        scores = [
            jnp.where(far_pos < limits[p], against(keys_v[p, :, lanes]), -1e30) for p in range(2)
        ]
        own_scores = jnp.where(own_seen, against(new_keys), -1e30)
        peak = jnp.maximum(
            jnp.maximum(
                jnp.max(scores[0], axis=1, keepdims=True), jnp.max(scores[1], axis=1, keepdims=True)
            ),
            jnp.max(own_scores, axis=1, keepdims=True),
        )
        weights = [jnp.exp(s - peak) for s in scores]
        own_weights = jnp.exp(own_scores - peak)
        total = (
            jnp.sum(weights[0], axis=1, keepdims=True)
            + jnp.sum(weights[1], axis=1, keepdims=True)
            + jnp.sum(own_weights, axis=1, keepdims=True)
        )
        scale = 1.0 / total
        attended = jnp.dot(
            (own_weights * scale).astype(jnp.bfloat16),
            new_values,
            preferred_element_type=jnp.float32,
        )
        for p in range(2):
            attended = attended + jnp.dot(
                (weights[p] * scale).astype(jnp.bfloat16),
                values_v[p, :, lanes],
                preferred_element_type=jnp.float32,
            )
        attended = attended.astype(jnp.bfloat16)
        for g in range(group_size):
            h = k * group_size + g
            gather_o[pl.ds(pl.multiple_of(me * ROWS, ROWS), ROWS), h * HD : (h + 1) * HD] = (
                attended[g * ROWS : (g + 1) * ROWS, :]
            )

    second = Gather(gather_o, 1)
    second.begin()
    scatter_sent(parts, own_parts, 0)
    loads[4].wait()
    for i in range(1, n):
        w_copy((me + i) % n, (me + i) % n).wait_recv()
    second.near_ready()
    cols[group_rows(near), :] = jnp.dot(
        gather_o[group_rows(near), :], w_cols[...], preferred_element_type=jnp.float32
    )
    scatter(cols, own_cols, 1, near, True)
    second.far_forward()
    second.far_ready()
    cols[group_rows(1 - near), :] = jnp.dot(
        gather_o[group_rows(1 - near), :], w_cols[...], preferred_element_type=jnp.float32
    )
    scatter(cols, own_cols, 1, 1 - near, False)
    second.finish()
    for i in range(1, n):
        w_copy((me + i) % n, (me + i) % n).wait_send()
    scatter_wait(cols, own_cols, 1)
    for j in range(n):
        lanes = slice(j * 128, (j + 1) * 128)
        hidden[:, lanes] = states[:, lanes] + own_cols[j * ROWS : (j + 1) * ROWS, :]
    block(gather_m, me)[...] = norm_rows(hidden[...], moe_gain[...]).astype(jnp.bfloat16)

    third = Gather(gather_m, 2)
    third.begin()
    scatter_sent(cols, own_cols, 1)
    loads[2].wait()
    loads[3].wait()
    ff = down_v.shape[0]

    def gate_up(group):
        @pl.loop(0, ff // 256)
        def _(t):
            at = pl.multiple_of(t * 256, 256)
            inputs = gather_m[group_rows(group), :]
            g = jnp.dot(
                inputs, gate_up_v[:, pl.ds(at, 256)], preferred_element_type=jnp.float32
            )
            u = jnp.dot(
                inputs,
                gate_up_v[:, pl.ds(pl.multiple_of(ff + t * 256, 256), 256)],
                preferred_element_type=jnp.float32,
            )
            act[:, pl.ds(at, 256)] = (g / (1.0 + jnp.exp(-g)) * u).astype(jnp.bfloat16)

    def down(group):
        @pl.loop(0, down_v.shape[1] // 512)
        def _(t):
            at = pl.multiple_of(t * 512, 512)
            expert_out[group_rows(group), pl.ds(at, 512)] = jnp.dot(
                act[...], down_v[:, pl.ds(at, 512)], preferred_element_type=jnp.float32
            ).astype(jnp.bfloat16)

    third.near_ready()
    gate_up(near)
    third.far_forward()
    down(near)
    scatter(expert_out, returned, 2, near, True)
    third.far_ready()
    gate_up(1 - near)
    down(1 - near)
    scatter(expert_out, returned, 2, 1 - near, False)
    third.finish()

    lane_at = lax.broadcasted_iota(jnp.int32, gates.shape, 1)

    def mixed(total, e):
        gate = jnp.sum(jnp.where(lane_at == e, gates[...], 0.0), axis=1, keepdims=True)
        got = block(returned, e)[...].astype(jnp.float32)
        return total + jnp.where(gate > 0.0, gate * got, 0.0)

    total = mixed(hidden[...], me)
    for group, start in ((near, 1), (1 - near, 0)):
        for i in range(start, half):
            e = group * half + (me + i) % half
            rdma(
                block(expert_out, e),
                block(returned, e),
                a2a_send.at[2, e],
                a2a_recv.at[2, e],
                e,
            ).wait_recv()
            total = mixed(total, e)
    out[...] = total
    scatter_sent(expert_out, returned, 2)


def tuned(
    states,
    attn_gain,
    moe_gain,
    w_query,
    w_key,
    w_value,
    w_output,
    w_gate_up,
    w_down,
    key_cache,
    value_cache,
    cache_lengths,
    prefix_slot,
    routes,
    gate_weights,
):
    n = lax.axis_size("ep")
    step_count, row_count, width = states.shape
    rows = step_count * row_count
    prefix_count, span, kv_width = key_cache.shape
    ff = w_down.shape[1]
    mine = prefix_slot[:, None] == jnp.arange(prefix_count)[None, :]
    limits = jnp.where(mine, cache_lengths[None, :], 0)
    positions = (
        jnp.sum(limits, axis=1).astype(jnp.float32)[None, :]
        + jnp.arange(step_count).astype(jnp.float32)[:, None]
    ).reshape(rows, 1)
    inverse_rate = THETA ** (-(jnp.arange(HD // 2).astype(jnp.float32) * 2.0 / HD))
    phases = positions * inverse_rate[None, :]
    cosine, sine = jnp.cos(phases), jnp.sin(phases)
    limits = jnp.tile(limits.astype(jnp.float32), (step_count, 1))
    aux = jnp.concatenate(
        [cosine, cosine, -sine, sine, jnp.pad(limits, ((0, 0), (0, 128 - prefix_count)))], axis=1
    )
    chosen = jnp.swapaxes(routes, 0, 1).reshape(rows, TOPK)
    gates = jnp.sum(
        jnp.where(
            chosen[:, :, None] == jnp.arange(128)[None, None, :],
            gate_weights.reshape(rows, TOPK)[:, :, None],
            0.0,
        ),
        axis=1,
    )
    in_vmem = pl.BlockSpec(memory_space=pltpu.VMEM)
    in_hbm = pl.BlockSpec(memory_space=pl.ANY)
    everyone = n * rows
    bf16, f32 = jnp.bfloat16, jnp.float32
    out, appended = pl.pallas_call(
        layer_kernel,
        out_shape=(
            jax.ShapeDtypeStruct((rows, width), f32),
            jax.ShapeDtypeStruct((rows, 2 * kv_width), bf16),
        ),
        in_specs=[in_vmem] * 8 + [in_hbm] * 5,
        out_specs=(in_vmem, in_vmem),
        scratch_shapes=[
            pltpu.VMEM((width, 256), bf16),
            pltpu.VMEM((everyone, width), bf16),
            pltpu.VMEM((everyone, width), bf16),
            pltpu.VMEM((everyone, width), bf16),
            pltpu.VMEM((everyone, 256), f32),
            pltpu.VMEM((everyone, 256), f32),
            pltpu.VMEM((width, 128), bf16),
            pltpu.VMEM((everyone, 128), f32),
            pltpu.VMEM((everyone, 128), f32),
            pltpu.VMEM((rows, width), f32),
            pltpu.VMEM((everyone // 2, ff), bf16),
            pltpu.VMEM((everyone, width), bf16),
            pltpu.VMEM((everyone, width), bf16),
            pltpu.VMEM((rows, kv_width), f32),
            pltpu.VMEM((rows, kv_width), f32),
            pltpu.VMEM((HQ * rows, HD), bf16),
            pltpu.VMEM((width, 2 * ff), bf16),
            pltpu.VMEM((ff, width), bf16),
            pltpu.VMEM((prefix_count, span, kv_width), bf16),
            pltpu.VMEM((prefix_count, span, kv_width), bf16),
            pltpu.SemaphoreType.DMA((5,)),
            pltpu.SemaphoreType.DMA((3, 16)),
            pltpu.SemaphoreType.DMA((3, 16)),
            pltpu.SemaphoreType.DMA((4, 16)),
            pltpu.SemaphoreType.DMA((4, 16)),
        ],
        compiler_params=pltpu.CompilerParams(
            collective_id=0, has_side_effects=True, vmem_limit_bytes=56 * 1024 * 1024
        ),
    )(
        states.reshape(rows, width),
        attn_gain.reshape(1, width),
        moe_gain.reshape(1, width),
        w_query,
        w_key,
        w_value,
        aux,
        gates,
        w_output,
        w_gate_up[0],
        w_down[0],
        key_cache,
        value_cache,
    )
    return (
        out.reshape(step_count, row_count, width),
        appended.reshape(step_count, row_count, 2 * kv_width),
    )


def solution(mesh):
    return jax.shard_map(
        tuned if mesh.shape["ep"] == TUNED_DEVICES else shards,
        mesh=mesh,
        in_specs=(
            P(None, ("groups", "ep"), None),
            P(),
            P(),
            P(None, "ep"),
            P(None, "ep"),
            P(None, "ep"),
            P("ep", None),
            P("ep", None, None),
            P("ep", None, None),
            P(("groups", "ep"), None, None),
            P(("groups", "ep"), None, None),
            P(("groups", "ep")),
            P(("groups", "ep")),
            P(("groups", "ep"), None, None),
            P(None, ("groups", "ep"), None),
        ),
        out_specs=(P(None, ("groups", "ep"), None), P(None, ("groups", "ep"), None)),
        check_vma=False,
    )
```

```python
import math

import jax
import jax.numpy as jnp
from jax import lax
from jax.experimental import pallas as pl
from jax.experimental.pallas import tpu as pltpu
from jax.sharding import PartitionSpec as P

HQ = 16
KVH = 2
HD = 128
TOPK = 8


EPS = 1e-06
THETA = 1000000.0


def rms_scale(values, gain):
    squares = jnp.mean(values * values, axis=-1, keepdims=True)
    return values * lax.rsqrt(squares + EPS) * gain


def rotate(vectors, positions):
    head_size = vectors.shape[-1]
    half_size = head_size // 2
    inverse_rate = THETA ** (-(jnp.arange(half_size).astype(jnp.float32) * 2.0 / head_size))
    phases = positions[..., None, None] * inverse_rate
    cosine = jnp.cos(phases)
    sine_part = jnp.sin(phases)
    first_half = vectors[..., :half_size]
    second_half = vectors[..., half_size:]
    return jnp.concatenate(
        [
            first_half * cosine - second_half * sine_part,
            second_half * cosine + first_half * sine_part,
        ],
        axis=-1,
    )


def attend_block(queries, new_keys, new_values, key_block, value_block, lengths, slots):
    step_count, row_count, head_count, head_size = queries.shape
    prefix_count, cache_span, kv_heads, _ = key_block.shape
    group_size = head_count // kv_heads
    grouped = queries.reshape(step_count, row_count, kv_heads, group_size, head_size)
    inv_root = 1.0 / math.sqrt(head_size)
    far_scores = (
        jnp.einsum("srkgd,pckd->srkgpc", grouped, key_block, preferred_element_type=jnp.float32)
        * inv_root
    )
    visible = (jnp.arange(cache_span)[None, None, :] < lengths[None, :, None]) & (
        slots[:, None, None] == jnp.arange(prefix_count)[None, :, None]
    )
    far_scores = jnp.where(visible[None, :, None, None], far_scores, -1e30)
    own_scores = (
        jnp.einsum("srkgd,trkd->srkgt", grouped, new_keys, preferred_element_type=jnp.float32)
        * inv_root
    )
    causal = jnp.arange(step_count)[None, :] <= jnp.arange(step_count)[:, None]
    own_scores = jnp.where(causal[:, None, None, None, :], own_scores, -1e30)
    peak = jnp.maximum(jnp.max(far_scores, axis=(-2, -1)), jnp.max(own_scores, axis=-1))
    far_weights = jnp.exp(far_scores - peak[..., None, None])
    own_weights = jnp.exp(own_scores - peak[..., None])
    normalizer = jnp.sum(far_weights, axis=(-2, -1)) + jnp.sum(own_weights, axis=-1)
    far_probs = (far_weights / normalizer[..., None, None]).astype(jnp.bfloat16)
    own_probs = (own_weights / normalizer[..., None]).astype(jnp.bfloat16)
    attended = jnp.einsum(
        "srkgpc,pckd->srkgd", far_probs, value_block, preferred_element_type=jnp.float32
    )
    attended = attended + jnp.einsum(
        "srkgt,trkd->srkgd", own_probs, new_values, preferred_element_type=jnp.float32
    )
    return attended.reshape(step_count, row_count, head_count * head_size).astype(jnp.bfloat16)


def shards(
    states,
    attn_gain,
    moe_gain,
    w_query,
    w_key,
    w_value,
    w_output,
    w_gate_up,
    w_down,
    key_cache,
    value_cache,
    cache_lengths,
    prefix_slot,
    routes,
    gate_weights,
):
    devices = lax.axis_size("ep")
    step_count, row_count, model_width = states.shape
    query_cols = w_query.shape[1]
    kv_cols = w_key.shape[1]
    normed = rms_scale(states, attn_gain).astype(jnp.bfloat16)
    joined = jnp.concatenate([w_query, w_key, w_value], axis=1)
    head_parts = jnp.einsum(
        "srd,dc->src",
        lax.all_gather(normed, "ep", axis=1, tiled=True),
        joined,
        preferred_element_type=jnp.float32,
    )
    own_cols = lax.all_to_all(head_parts, "ep", split_axis=1, concat_axis=2, tiled=True)
    own_cols = own_cols.reshape(step_count, row_count, devices, query_cols + 2 * kv_cols)
    queries = own_cols[..., :query_cols].reshape(step_count, row_count, HQ, HD)
    new_keys = own_cols[..., query_cols : query_cols + kv_cols].reshape(
        step_count, row_count, KVH, HD
    )
    new_values = (
        own_cols[..., query_cols + kv_cols :]
        .reshape(step_count, row_count, KVH, HD)
        .astype(jnp.bfloat16)
    )
    prefix_count, cache_span, _ = key_cache.shape
    lengths_here = jnp.sum(
        jnp.where(
            prefix_slot[:, None] == jnp.arange(prefix_count)[None, :], cache_lengths[None, :], 0
        ),
        axis=1,
    )
    positions = (
        lengths_here.astype(jnp.float32)[None, :]
        + jnp.arange(step_count).astype(jnp.float32)[:, None]
    )
    queries = rotate(queries, positions).astype(jnp.bfloat16)
    new_keys = rotate(new_keys, positions).astype(jnp.bfloat16)
    attended = attend_block(
        queries,
        new_keys,
        new_values,
        key_cache.reshape(prefix_count, cache_span, KVH, HD),
        value_cache.reshape(prefix_count, cache_span, KVH, HD),
        cache_lengths,
        prefix_slot,
    )
    w_columns = lax.all_to_all(w_output, "ep", split_axis=1, concat_axis=0, tiled=True)
    column_part = jnp.einsum(
        "srf,fc->src",
        lax.all_gather(attended, "ep", axis=1, tiled=True),
        w_columns,
        preferred_element_type=jnp.float32,
    )
    projected = lax.all_to_all(column_part, "ep", split_axis=1, concat_axis=2, tiled=True)
    hidden = states + projected
    moe_input = (
        rms_scale(hidden, moe_gain)
        .astype(jnp.bfloat16)
        .reshape(step_count * row_count, model_width)
    )
    expert_count = w_gate_up.shape[0] * devices
    capacity = max(2, 4 * row_count * TOPK // expert_count)
    flat_routes = jnp.swapaxes(routes, 0, 1).reshape(-1)
    onehot = (flat_routes[:, None] == jnp.arange(expert_count)[None, :]).astype(jnp.int32)
    running = jnp.cumsum(onehot, axis=0) - 1
    within = jnp.sum(onehot * running, axis=1)
    slot_index = flat_routes * capacity + within
    dispatch = (jnp.arange(expert_count * capacity)[:, None] == slot_index[None, :]).astype(
        jnp.bfloat16
    )
    repeated = jnp.repeat(moe_input, TOPK, axis=0)
    outgoing = jnp.dot(dispatch, repeated, preferred_element_type=jnp.float32).astype(jnp.bfloat16)
    outgoing = outgoing.reshape(expert_count, capacity, model_width)
    both = jnp.einsum(
        "nsd,df->nsf",
        lax.all_to_all(outgoing, "ep", split_axis=0, concat_axis=0, tiled=True),
        w_gate_up[0],
        preferred_element_type=jnp.float32,
    )
    half_cols = both.shape[-1] // 2
    activation = (jax.nn.silu(both[..., :half_cols]) * both[..., half_cols:]).astype(jnp.bfloat16)
    expert_done = jnp.einsum(
        "nsf,fd->nsd", activation, w_down[0], preferred_element_type=jnp.float32
    ).astype(jnp.bfloat16)
    returned = lax.all_to_all(expert_done, "ep", split_axis=0, concat_axis=0, tiled=True)
    picked = returned.reshape(expert_count * capacity, model_width)[slot_index]
    picked = picked.astype(jnp.float32).reshape(step_count, row_count, TOPK, model_width)
    mixture = jnp.sum(gate_weights[..., None] * picked, axis=2)
    appended = jnp.concatenate(
        [
            new_keys.reshape(step_count, row_count, KVH * HD),
            new_values.reshape(step_count, row_count, KVH * HD),
        ],
        axis=-1,
    )
    return (hidden + mixture, appended)


TUNED_DEVICES = 16
ROWS = 16


def norm_rows(values, gain):
    squares = jnp.mean(values * values, axis=-1, keepdims=True)
    return values * lax.rsqrt(squares + EPS) * gain


def layer_kernel(
    states,
    attn_gain,
    moe_gain,
    rates,
    lengths,
    slots,
    routes,
    gate_weights,
    w_query,
    w_key,
    w_value,
    w_output,
    w_gate_up,
    w_down,
    key_cache,
    value_cache,
    out,
    appended,
    w_query_v,
    w_kv_v,
    gates,
    mirror_gates,
    relay,
    summed,
    from_mirror,
    gather_q,
    gather_o,
    gather_m,
    parts,
    own_parts,
    w_cols,
    cols,
    own_cols,
    hidden,
    act,
    expert_out,
    returned,
    fresh_k,
    fresh_v,
    queries,
    gate_up_v,
    down_v,
    keys_v,
    values_v,
    load_sem,
    ag_send,
    ag_recv,
    a2a_send,
    a2a_recv,
):
    n = TUNED_DEVICES
    half = n // 2
    me = lax.axis_index("ep")
    c = me % 2
    y = (me // 2) % 2
    z = me // 4
    near = me // half
    z_pair = z + 1 - 2 * (z % 2)
    mirror = (me + half) % n

    def index_of(zz, yy, cc):
        return (zz * 2 + yy) * 2 + cc

    def block(ref, i, rows=ROWS):
        if len(ref.shape) == 3:
            return ref.at[i]
        return ref.at[pl.ds(pl.multiple_of(i * rows, rows), rows), :]

    def rdma(src, dst, send, recv, target):
        return pltpu.make_async_remote_copy(
            src_ref=src,
            dst_ref=dst,
            send_sem=send,
            recv_sem=recv,
            device_id={"ep": target},
            device_id_type=pl.DeviceIdType.MESH,
        )

    barrier = pltpu.get_barrier_semaphore()
    for i in range(1, n):
        pl.semaphore_signal(
            barrier,
            inc=1,
            device_id={"ep": (me + i) % n},
            device_id_type=pl.DeviceIdType.MESH,
        )

    loads = [
        pltpu.make_async_copy(key_cache, keys_v, load_sem.at[0]),
        pltpu.make_async_copy(value_cache, values_v, load_sem.at[1]),
        pltpu.make_async_copy(w_gate_up, gate_up_v, load_sem.at[2]),
        pltpu.make_async_copy(w_down, down_v, load_sem.at[3]),
        pltpu.make_async_copy(
            w_output.at[:, pl.ds(pl.multiple_of(me * 128, 128), 128)],
            block(w_cols, me, 128),
            load_sem.at[4],
        ),
        pltpu.make_async_copy(w_query, w_query_v, load_sem.at[5]),
        pltpu.make_async_copy(w_key, w_kv_v.at[0:16, :], load_sem.at[6]),
        pltpu.make_async_copy(w_value, w_kv_v.at[16:32, :], load_sem.at[7]),
    ]
    for i in (5, 6, 7, 0, 1, 4, 2, 3):
        loads[i].start()

    class Gather:
        def __init__(self, buf, phase):
            self.buf, self.phase, self.sends = buf, phase, []

        def push(self, src, target):
            k = len(self.sends)
            copy = rdma(
                block(self.buf, src),
                block(self.buf, src),
                ag_send.at[self.phase, k],
                ag_recv.at[self.phase, src],
                target,
            )
            copy.start()
            self.sends.append(copy)

        def arrived(self, src):
            rdma(
                block(self.buf, src),
                block(self.buf, src),
                ag_send.at[self.phase, 0],
                ag_recv.at[self.phase, src],
                index_of(z, y, 1 - c),
            ).wait_recv()

        def spread(self, src):
            self.push(src, index_of(z, 1 - y, c))
            self.push(src, index_of(z_pair, y, c))
            self.push(src, index_of(z, y, 1 - c))

        def begin(self):
            self.push(me, mirror)
            self.spread(me)

        def from_y(self, zz, shift):
            src = (index_of(zz, 1 - y, c) + shift) % n
            self.arrived(src)
            self.push(src, index_of(z, y, 1 - c))

        def from_z(self, shift):
            src = (index_of(z_pair, y, c) + shift) % n
            self.arrived(src)
            self.push(src, index_of(z, 1 - y, c))
            self.push(src, index_of(z, y, 1 - c))

        def ready(self, shift):
            self.from_z(shift)
            self.from_y(z, shift)
            if shift == 0:
                self.arrived(mirror)
                self.spread(mirror)
            self.from_y(z_pair, shift)
            for zz in (z, z_pair):
                for yy in (y, 1 - y):
                    self.arrived((index_of(zz, yy, 1 - c) + shift) % n)

        def finish(self):
            for copy in self.sends:
                copy.wait_send()

    def scatter(src, dst, phase, group, is_near):
        first = 1 if is_near else 0
        for i in range(first, half):
            p = group * half + (me + i) % half
            rdma(
                block(src, p),
                block(dst, me),
                a2a_send.at[phase, p],
                a2a_recv.at[phase, me],
                p,
            ).start()
        if is_near:
            block(dst, me)[...] = block(src, me)[...]

    def scatter_wait(src, dst, phase, rows=ROWS):
        for i in range(1, n):
            p = (me + i) % n
            rdma(
                block(src, p, rows),
                block(dst, p, rows),
                a2a_send.at[phase, p],
                a2a_recv.at[phase, p],
                p,
            ).wait_recv()

    def scatter_sent(src, dst, phase):
        for i in range(1, n):
            p = (me + i) % n
            rdma(
                block(src, p),
                block(dst, p),
                a2a_send.at[phase, p],
                a2a_recv.at[phase, p],
                p,
            ).wait_send()

    def w_copy(p, landing):
        return rdma(
            w_output.at[:, pl.ds(pl.multiple_of(p * 128, 128), 128)],
            block(w_cols, landing, 128),
            a2a_send.at[3, p],
            a2a_recv.at[3, landing],
            p,
        )

    block(gather_q, me)[...] = norm_rows(states[...], attn_gain[...]).astype(jnp.bfloat16)
    pl.semaphore_wait(barrier, n - 1)

    first = Gather(gather_q, 0)
    first.begin()
    row_id = lax.broadcasted_iota(jnp.int32, (ROWS, 128), 0)
    lane_id = lax.broadcasted_iota(jnp.int32, (ROWS, 128), 1)
    chosen = jnp.concatenate([routes[:, 0, :], routes[:, 1, :]], axis=0)
    shares = jnp.concatenate([gate_weights[0], gate_weights[1]], axis=0)
    weighed = jnp.zeros((ROWS, 128), jnp.float32)
    for k in range(TOPK):
        weighed = jnp.where(lane_id == chosen[:, k : k + 1], shares[:, k : k + 1], weighed)
    gates[...] = weighed
    gates_copy = rdma(gates, mirror_gates, a2a_send.at[5, 1], a2a_recv.at[5, 1], mirror)
    gates_copy.start()
    slot_of = jnp.zeros((ROWS, 128), jnp.int32)
    for b in range(8):
        slot_of = jnp.where(row_id % 8 == b, slots[b], slot_of)
    limits = [jnp.where(slot_of == p, lengths[p], 0) for p in range(2)]
    phases = (limits[0] + limits[1] + row_id // 8).astype(jnp.float32) * rates[...]
    cosine = jnp.cos(phases)
    sine = jnp.sin(phases)
    sine = jnp.where(lane_id < 64, -sine, sine)

    def group_rows(group):
        return pl.ds(pl.multiple_of(group * 128, 128), 128)

    first.ready(0)
    for i in (5, 6, 7):
        loads[i].wait()

    def project(group):
        inputs = gather_q[group_rows(group), :]
        q = jnp.dot(inputs, w_query_v[...], preferred_element_type=jnp.float32)
        kv = lax.dot_general(
            inputs, w_kv_v[...], (((1,), (1,)), ((), ())), preferred_element_type=jnp.float32
        )
        kv = kv.reshape(half, ROWS, 32)
        kv = jnp.concatenate([kv[:, 4 * a : 4 * a + 4, :] for a in range(4)], axis=-1)
        parts[pl.ds(group * half, half), 0:ROWS, :] = q.reshape(half, ROWS, 128)
        parts[pl.ds(group * half, half), ROWS : ROWS + 4, :] = kv
        parts[pl.ds(group * half, half), ROWS + 4 : ROWS + 8, :] = jnp.zeros_like(kv)

    project(near)
    scatter(parts, own_parts, 0, near, True)
    first.ready(half)
    project(1 - near)
    scatter(parts, own_parts, 0, 1 - near, False)
    for i in range(1, n):
        w_copy((me + i) % n, me).start()
    first.finish()
    scatter_wait(parts, own_parts, 0)

    def turned(vectors):
        return vectors * cosine + pltpu.roll(vectors, 64, 1) * sine

    for j in range(n):
        rows = slice(j * ROWS, (j + 1) * ROWS)
        queries[rows, :] = turned(own_parts[j, 0:ROWS, :]).astype(jnp.bfloat16)
        packed = own_parts[j, ROWS : ROWS + 4, :]
        unpacked = jnp.concatenate([packed[:, 32 * a : 32 * a + 32] for a in range(4)], axis=0)
        fresh_k[:, j * 16 : (j + 1) * 16] = unpacked[:, 0:16]
        fresh_v[:, j * 16 : (j + 1) * 16] = unpacked[:, 16:32]
    loads[0].wait()
    loads[1].wait()
    inv_root = 1.0 / math.sqrt(HD)
    group_size = HQ // KVH
    q_rows = group_size * ROWS
    span = keys_v.shape[1]
    far_pos = lax.broadcasted_iota(jnp.int32, (q_rows, span), 1)
    row_at = lax.broadcasted_iota(jnp.int32, (q_rows, ROWS), 0) % ROWS
    col_at = lax.broadcasted_iota(jnp.int32, (q_rows, ROWS), 1)
    own_seen = (row_at % 8 == col_at % 8) & (col_at // 8 <= row_at // 8)
    limits = [jnp.concatenate([m[:, 0:1]] * group_size, axis=0) for m in limits]
    for k in range(KVH):
        lanes = slice(k * HD, (k + 1) * HD)
        new_keys = turned(fresh_k[:, lanes]).astype(jnp.bfloat16)
        new_values = fresh_v[:, lanes].astype(jnp.bfloat16)
        appended[:, lanes] = new_keys
        appended[:, slice((KVH + k) * HD, (KVH + k + 1) * HD)] = new_values
        q = queries[k * q_rows : (k + 1) * q_rows, :]

        def against(rows):
            return (
                lax.dot_general(
                    q, rows, (((1,), (1,)), ((), ())), preferred_element_type=jnp.float32
                )
                * inv_root
            )

        scores = [
            jnp.where(far_pos < limits[p], against(keys_v[p, :, lanes]), -1e30) for p in range(2)
        ]
        own_scores = jnp.where(own_seen, against(new_keys), -1e30)
        peak = jnp.maximum(
            jnp.maximum(
                jnp.max(scores[0], axis=1, keepdims=True), jnp.max(scores[1], axis=1, keepdims=True)
            ),
            jnp.max(own_scores, axis=1, keepdims=True),
        )
        weights = [jnp.exp(s - peak) for s in scores]
        own_weights = jnp.exp(own_scores - peak)
        total = (
            jnp.sum(weights[0], axis=1, keepdims=True)
            + jnp.sum(weights[1], axis=1, keepdims=True)
            + jnp.sum(own_weights, axis=1, keepdims=True)
        )
        scale = 1.0 / total
        attended = jnp.dot(
            (own_weights * scale).astype(jnp.bfloat16),
            new_values,
            preferred_element_type=jnp.float32,
        )
        for p in range(2):
            attended = attended + jnp.dot(
                (weights[p] * scale).astype(jnp.bfloat16),
                values_v[p, :, lanes],
                preferred_element_type=jnp.float32,
            )
        attended = attended.astype(jnp.bfloat16)
        for g in range(group_size):
            h = k * group_size + g
            gather_o[pl.ds(pl.multiple_of(me * ROWS, ROWS), ROWS), h * HD : (h + 1) * HD] = (
                attended[g * ROWS : (g + 1) * ROWS, :]
            )

    second = Gather(gather_o, 1)
    second.begin()
    scatter_sent(parts, own_parts, 0)
    loads[4].wait()
    for i in range(1, n):
        w_copy((me + i) % n, (me + i) % n).wait_recv()
    second.ready(0)
    cols[group_rows(near), :] = jnp.dot(
        gather_o[group_rows(near), :], w_cols[...], preferred_element_type=jnp.float32
    )
    scatter(cols, own_cols, 1, near, True)
    second.ready(half)
    cols[group_rows(1 - near), :] = jnp.dot(
        gather_o[group_rows(1 - near), :], w_cols[...], preferred_element_type=jnp.float32
    )
    scatter(cols, own_cols, 1, 1 - near, False)
    second.finish()
    for i in range(1, n):
        w_copy((me + i) % n, (me + i) % n).wait_send()
    scatter_wait(cols, own_cols, 1)
    for j in range(n):
        lanes = slice(j * 128, (j + 1) * 128)
        hidden[:, lanes] = states[:, lanes] + own_cols[j * ROWS : (j + 1) * ROWS, :]
    block(gather_m, me)[...] = norm_rows(hidden[...], moe_gain[...]).astype(jnp.bfloat16)

    third = Gather(gather_m, 2)
    third.begin()
    scatter_sent(cols, own_cols, 1)
    loads[2].wait()
    loads[3].wait()
    ff = down_v.shape[0]

    def gate_up(group):
        @pl.loop(0, ff // 256)
        def _(t):
            at = pl.multiple_of(t * 256, 256)
            inputs = gather_m[group_rows(group), :]
            g = jnp.dot(
                inputs, gate_up_v[:, pl.ds(at, 256)], preferred_element_type=jnp.float32
            )
            u = jnp.dot(
                inputs,
                gate_up_v[:, pl.ds(pl.multiple_of(ff + t * 256, 256), 256)],
                preferred_element_type=jnp.float32,
            )
            act[:, pl.ds(at, 256)] = (g / (1.0 + jnp.exp(-g)) * u).astype(jnp.bfloat16)

    def down(group):
        @pl.loop(0, down_v.shape[1] // 512)
        def _(t):
            at = pl.multiple_of(t * 512, 512)
            expert_out[group_rows(group), pl.ds(at, 512)] = jnp.dot(
                act[...], down_v[:, pl.ds(at, 512)], preferred_element_type=jnp.float32
            ).astype(jnp.bfloat16)

    third.ready(0)
    gate_up(near)
    down(near)
    for i in range(1, half):
        mate = near * half + (me + i) % half
        rdma(
            block(expert_out, mate),
            block(returned, me % half),
            a2a_send.at[2, mate],
            a2a_recv.at[2, me],
            mate,
        ).start()
    third.ready(half)
    gate_up(1 - near)
    down(1 - near)
    for i in range(1, half):
        mate = near * half + (me + i) % half
        rdma(
            block(expert_out, (mate + half) % n),
            block(relay, me % half),
            a2a_send.at[4, mate],
            a2a_recv.at[4, me],
            mate,
        ).start()
    third.finish()

    def mixed(total, shares, e, got):
        share = jnp.sum(jnp.where(lane_id == e, shares[...], 0.0), axis=1, keepdims=True)
        return total + jnp.where(share > 0.0, share * got[...].astype(jnp.float32), 0.0)

    def mix(total, shares, phase, buf):
        for i in range(1, half):
            e = near * half + (me + i) % half
            rdma(
                block(expert_out, e),
                block(buf, e % half),
                a2a_send.at[phase, e],
                a2a_recv.at[phase, e],
                e,
            ).wait_recv()
            total = mixed(total, shares, e, block(buf, e % half))
        return total

    gates_copy.wait()
    total = mixed(jnp.zeros(hidden.shape, jnp.float32), mirror_gates, me, block(expert_out, mirror))
    summed[...] = mix(total, mirror_gates, 4, relay)
    sum_copy = rdma(summed, from_mirror, a2a_send.at[5, 0], a2a_recv.at[5, 0], mirror)
    sum_copy.start()
    total = mixed(hidden[...], gates, me, block(expert_out, me))
    total = mix(total, gates, 2, returned)
    sum_copy.wait()
    out[...] = total + from_mirror[...]
    for phase, buf in ((2, returned), (4, relay)):
        for i in range(1, half):
            e = near * half + (me + i) % half
            rdma(
                block(expert_out, e),
                block(buf, e % half),
                a2a_send.at[phase, e],
                a2a_recv.at[phase, e],
                e,
            ).wait_send()


def tuned(
    states,
    attn_gain,
    moe_gain,
    w_query,
    w_key,
    w_value,
    w_output,
    w_gate_up,
    w_down,
    key_cache,
    value_cache,
    cache_lengths,
    prefix_slot,
    routes,
    gate_weights,
):
    n = lax.axis_size("ep")
    step_count, row_count, width = states.shape
    rows = step_count * row_count
    prefix_count, span, kv_width = key_cache.shape
    ff = w_down.shape[1]
    inverse_rate = THETA ** (-(jnp.arange(HD // 2).astype(jnp.float32) * 2.0 / HD))
    rates = jnp.tile(inverse_rate, 2).reshape(1, HD)
    in_vmem = pl.BlockSpec(memory_space=pltpu.VMEM)
    in_smem = pl.BlockSpec(memory_space=pltpu.SMEM)
    in_hbm = pl.BlockSpec(memory_space=pl.ANY)
    everyone = n * rows
    bf16, f32 = jnp.bfloat16, jnp.float32
    out, appended = pl.pallas_call(
        layer_kernel,
        out_shape=(
            jax.ShapeDtypeStruct((rows, width), f32),
            jax.ShapeDtypeStruct((rows, 2 * kv_width), bf16),
        ),
        in_specs=[in_vmem] * 4 + [in_smem] * 2 + [in_vmem] * 2 + [in_hbm] * 8,
        out_specs=(in_vmem, in_vmem),
        scratch_shapes=[
            pltpu.VMEM((width, 128), bf16),
            pltpu.VMEM((32, width), bf16),
            pltpu.VMEM((rows, 128), f32),
            pltpu.VMEM((rows, 128), f32),
            pltpu.VMEM((everyone // 2, width), bf16),
            pltpu.VMEM((rows, width), f32),
            pltpu.VMEM((rows, width), f32),
            pltpu.VMEM((everyone, width), bf16),
            pltpu.VMEM((everyone, width), bf16),
            pltpu.VMEM((everyone, width), bf16),
            pltpu.VMEM((n, rows + 8, 128), f32),
            pltpu.VMEM((n, rows + 8, 128), f32),
            pltpu.VMEM((width, 128), bf16),
            pltpu.VMEM((everyone, 128), f32),
            pltpu.VMEM((everyone, 128), f32),
            pltpu.VMEM((rows, width), f32),
            pltpu.VMEM((everyone // 2, ff), bf16),
            pltpu.VMEM((everyone, width), bf16),
            pltpu.VMEM((everyone // 2, width), bf16),
            pltpu.VMEM((rows, kv_width), f32),
            pltpu.VMEM((rows, kv_width), f32),
            pltpu.VMEM((HQ * rows, HD), bf16),
            pltpu.VMEM((width, 2 * ff), bf16),
            pltpu.VMEM((ff, width), bf16),
            pltpu.VMEM((prefix_count, span, kv_width), bf16),
            pltpu.VMEM((prefix_count, span, kv_width), bf16),
            pltpu.SemaphoreType.DMA((8,)),
            pltpu.SemaphoreType.DMA((3, 16)),
            pltpu.SemaphoreType.DMA((3, 16)),
            pltpu.SemaphoreType.DMA((6, 16)),
            pltpu.SemaphoreType.DMA((6, 16)),
        ],
        compiler_params=pltpu.CompilerParams(
            collective_id=0, has_side_effects=True, vmem_limit_bytes=56 * 1024 * 1024
        ),
    )(
        states.reshape(rows, width),
        attn_gain.reshape(1, width),
        moe_gain.reshape(1, width),
        rates,
        cache_lengths,
        prefix_slot,
        routes,
        gate_weights,
        w_query,
        w_key.T,
        w_value.T,
        w_output,
        w_gate_up[0],
        w_down[0],
        key_cache,
        value_cache,
    )
    return (
        out.reshape(step_count, row_count, width),
        appended.reshape(step_count, row_count, 2 * kv_width),
    )


def solution(mesh):
    return jax.shard_map(
        tuned if mesh.shape["ep"] == TUNED_DEVICES else shards,
        mesh=mesh,
        in_specs=(
            P(None, ("groups", "ep"), None),
            P(),
            P(),
            P(None, "ep"),
            P(None, "ep"),
            P(None, "ep"),
            P("ep", None),
            P("ep", None, None),
            P("ep", None, None),
            P(("groups", "ep"), None, None),
            P(("groups", "ep"), None, None),
            P(("groups", "ep")),
            P(("groups", "ep")),
            P(("groups", "ep"), None, None),
            P(None, ("groups", "ep"), None),
        ),
        out_specs=(P(None, ("groups", "ep"), None), P(None, ("groups", "ep"), None)),
        check_vma=False,
    )
```

```python
import math

import jax
import jax.numpy as jnp
from jax import lax
from jax.experimental import pallas as pl
from jax.experimental.pallas import tpu as pltpu
from jax.sharding import PartitionSpec as P

HQ = 16
KVH = 2
HD = 128
TOPK = 8


EPS = 1e-06
THETA = 1000000.0


def rms_scale(values, gain):
    squares = jnp.mean(values * values, axis=-1, keepdims=True)
    return values * lax.rsqrt(squares + EPS) * gain


def rotate(vectors, positions):
    head_size = vectors.shape[-1]
    half_size = head_size // 2
    inverse_rate = THETA ** (-(jnp.arange(half_size).astype(jnp.float32) * 2.0 / head_size))
    phases = positions[..., None, None] * inverse_rate
    cosine = jnp.cos(phases)
    sine_part = jnp.sin(phases)
    first_half = vectors[..., :half_size]
    second_half = vectors[..., half_size:]
    return jnp.concatenate(
        [
            first_half * cosine - second_half * sine_part,
            second_half * cosine + first_half * sine_part,
        ],
        axis=-1,
    )


def attend_block(queries, new_keys, new_values, key_block, value_block, lengths, slots):
    step_count, row_count, head_count, head_size = queries.shape
    prefix_count, cache_span, kv_heads, _ = key_block.shape
    group_size = head_count // kv_heads
    grouped = queries.reshape(step_count, row_count, kv_heads, group_size, head_size)
    inv_root = 1.0 / math.sqrt(head_size)
    far_scores = (
        jnp.einsum("srkgd,pckd->srkgpc", grouped, key_block, preferred_element_type=jnp.float32)
        * inv_root
    )
    visible = (jnp.arange(cache_span)[None, None, :] < lengths[None, :, None]) & (
        slots[:, None, None] == jnp.arange(prefix_count)[None, :, None]
    )
    far_scores = jnp.where(visible[None, :, None, None], far_scores, -1e30)
    own_scores = (
        jnp.einsum("srkgd,trkd->srkgt", grouped, new_keys, preferred_element_type=jnp.float32)
        * inv_root
    )
    causal = jnp.arange(step_count)[None, :] <= jnp.arange(step_count)[:, None]
    own_scores = jnp.where(causal[:, None, None, None, :], own_scores, -1e30)
    peak = jnp.maximum(jnp.max(far_scores, axis=(-2, -1)), jnp.max(own_scores, axis=-1))
    far_weights = jnp.exp(far_scores - peak[..., None, None])
    own_weights = jnp.exp(own_scores - peak[..., None])
    normalizer = jnp.sum(far_weights, axis=(-2, -1)) + jnp.sum(own_weights, axis=-1)
    far_probs = (far_weights / normalizer[..., None, None]).astype(jnp.bfloat16)
    own_probs = (own_weights / normalizer[..., None]).astype(jnp.bfloat16)
    attended = jnp.einsum(
        "srkgpc,pckd->srkgd", far_probs, value_block, preferred_element_type=jnp.float32
    )
    attended = attended + jnp.einsum(
        "srkgt,trkd->srkgd", own_probs, new_values, preferred_element_type=jnp.float32
    )
    return attended.reshape(step_count, row_count, head_count * head_size).astype(jnp.bfloat16)


def shards(
    states,
    attn_gain,
    moe_gain,
    w_query,
    w_key,
    w_value,
    w_output,
    w_gate_up,
    w_down,
    key_cache,
    value_cache,
    cache_lengths,
    prefix_slot,
    routes,
    gate_weights,
):
    devices = lax.axis_size("ep")
    step_count, row_count, model_width = states.shape
    query_cols = w_query.shape[1]
    kv_cols = w_key.shape[1]
    normed = rms_scale(states, attn_gain).astype(jnp.bfloat16)
    joined = jnp.concatenate([w_query, w_key, w_value], axis=1)
    head_parts = jnp.einsum(
        "srd,dc->src",
        lax.all_gather(normed, "ep", axis=1, tiled=True),
        joined,
        preferred_element_type=jnp.float32,
    )
    own_cols = lax.all_to_all(head_parts, "ep", split_axis=1, concat_axis=2, tiled=True)
    own_cols = own_cols.reshape(step_count, row_count, devices, query_cols + 2 * kv_cols)
    queries = own_cols[..., :query_cols].reshape(step_count, row_count, HQ, HD)
    new_keys = own_cols[..., query_cols : query_cols + kv_cols].reshape(
        step_count, row_count, KVH, HD
    )
    new_values = (
        own_cols[..., query_cols + kv_cols :]
        .reshape(step_count, row_count, KVH, HD)
        .astype(jnp.bfloat16)
    )
    prefix_count, cache_span, _ = key_cache.shape
    lengths_here = jnp.sum(
        jnp.where(
            prefix_slot[:, None] == jnp.arange(prefix_count)[None, :], cache_lengths[None, :], 0
        ),
        axis=1,
    )
    positions = (
        lengths_here.astype(jnp.float32)[None, :]
        + jnp.arange(step_count).astype(jnp.float32)[:, None]
    )
    queries = rotate(queries, positions).astype(jnp.bfloat16)
    new_keys = rotate(new_keys, positions).astype(jnp.bfloat16)
    attended = attend_block(
        queries,
        new_keys,
        new_values,
        key_cache.reshape(prefix_count, cache_span, KVH, HD),
        value_cache.reshape(prefix_count, cache_span, KVH, HD),
        cache_lengths,
        prefix_slot,
    )
    w_columns = lax.all_to_all(w_output, "ep", split_axis=1, concat_axis=0, tiled=True)
    column_part = jnp.einsum(
        "srf,fc->src",
        lax.all_gather(attended, "ep", axis=1, tiled=True),
        w_columns,
        preferred_element_type=jnp.float32,
    )
    projected = lax.all_to_all(column_part, "ep", split_axis=1, concat_axis=2, tiled=True)
    hidden = states + projected
    moe_input = (
        rms_scale(hidden, moe_gain)
        .astype(jnp.bfloat16)
        .reshape(step_count * row_count, model_width)
    )
    expert_count = w_gate_up.shape[0] * devices
    capacity = max(2, 4 * row_count * TOPK // expert_count)
    flat_routes = jnp.swapaxes(routes, 0, 1).reshape(-1)
    onehot = (flat_routes[:, None] == jnp.arange(expert_count)[None, :]).astype(jnp.int32)
    running = jnp.cumsum(onehot, axis=0) - 1
    within = jnp.sum(onehot * running, axis=1)
    slot_index = flat_routes * capacity + within
    dispatch = (jnp.arange(expert_count * capacity)[:, None] == slot_index[None, :]).astype(
        jnp.bfloat16
    )
    repeated = jnp.repeat(moe_input, TOPK, axis=0)
    outgoing = jnp.dot(dispatch, repeated, preferred_element_type=jnp.float32).astype(jnp.bfloat16)
    outgoing = outgoing.reshape(expert_count, capacity, model_width)
    both = jnp.einsum(
        "nsd,df->nsf",
        lax.all_to_all(outgoing, "ep", split_axis=0, concat_axis=0, tiled=True),
        w_gate_up[0],
        preferred_element_type=jnp.float32,
    )
    half_cols = both.shape[-1] // 2
    activation = (jax.nn.silu(both[..., :half_cols]) * both[..., half_cols:]).astype(jnp.bfloat16)
    expert_done = jnp.einsum(
        "nsf,fd->nsd", activation, w_down[0], preferred_element_type=jnp.float32
    ).astype(jnp.bfloat16)
    returned = lax.all_to_all(expert_done, "ep", split_axis=0, concat_axis=0, tiled=True)
    picked = returned.reshape(expert_count * capacity, model_width)[slot_index]
    picked = picked.astype(jnp.float32).reshape(step_count, row_count, TOPK, model_width)
    mixture = jnp.sum(gate_weights[..., None] * picked, axis=2)
    appended = jnp.concatenate(
        [
            new_keys.reshape(step_count, row_count, KVH * HD),
            new_values.reshape(step_count, row_count, KVH * HD),
        ],
        axis=-1,
    )
    return (hidden + mixture, appended)


TUNED_DEVICES = 16
ROWS = 16


def norm_rows(values, gain):
    squares = jnp.mean(values * values, axis=-1, keepdims=True)
    return values * lax.rsqrt(squares + EPS) * gain


def layer_kernel(
    states,
    attn_gain,
    moe_gain,
    rates,
    lengths,
    slots,
    routes,
    gate_weights,
    w_query,
    w_key,
    w_value,
    w_output,
    w_gate_up,
    w_down,
    key_cache,
    value_cache,
    out,
    appended,
    w_query_v,
    w_kv_v,
    gates,
    mirror_gates,
    relay,
    summed,
    from_mirror,
    gather_q,
    gather_o,
    gather_m,
    parts,
    own_parts,
    w_cols,
    cols,
    own_cols,
    hidden,
    act,
    expert_out,
    returned,
    fresh_k,
    fresh_v,
    queries,
    gate_up_v,
    down_v,
    keys_v,
    values_v,
    load_sem,
    ag_send,
    ag_recv,
    a2a_send,
    a2a_recv,
):
    n = TUNED_DEVICES
    half = n // 2
    me = lax.axis_index("ep")
    c = me % 2
    y = (me // 2) % 2
    z = me // 4
    near = me // half
    z_pair = z + 1 - 2 * (z % 2)
    mirror = (me + half) % n

    def index_of(zz, yy, cc):
        return (zz * 2 + yy) * 2 + cc

    def block(ref, i, rows=ROWS):
        if len(ref.shape) == 3:
            return ref.at[i]
        return ref.at[pl.ds(pl.multiple_of(i * rows, rows), rows), :]

    def rdma(src, dst, send, recv, target):
        return pltpu.make_async_remote_copy(
            src_ref=src,
            dst_ref=dst,
            send_sem=send,
            recv_sem=recv,
            device_id={"ep": target},
            device_id_type=pl.DeviceIdType.MESH,
        )

    barrier = pltpu.get_barrier_semaphore()
    for i in range(1, n):
        pl.semaphore_signal(
            barrier,
            inc=1,
            device_id={"ep": (me + i) % n},
            device_id_type=pl.DeviceIdType.MESH,
        )

    loads = [
        pltpu.make_async_copy(key_cache, keys_v, load_sem.at[0]),
        pltpu.make_async_copy(value_cache, values_v, load_sem.at[1]),
        pltpu.make_async_copy(w_gate_up, gate_up_v, load_sem.at[2]),
        pltpu.make_async_copy(w_down, down_v, load_sem.at[3]),
        pltpu.make_async_copy(
            w_output.at[:, pl.ds(pl.multiple_of(me * 128, 128), 128)],
            block(w_cols, me, 128),
            load_sem.at[4],
        ),
        pltpu.make_async_copy(w_query, w_query_v, load_sem.at[5]),
        pltpu.make_async_copy(w_key, w_kv_v.at[0:16, :], load_sem.at[6]),
        pltpu.make_async_copy(w_value, w_kv_v.at[16:32, :], load_sem.at[7]),
    ]
    for i in (5, 6, 7, 0, 1, 4, 2, 3):
        loads[i].start()

    class Gather:
        def __init__(self, buf, phase):
            self.buf, self.phase, self.sends = buf, phase, []

        def push(self, src, target):
            k = len(self.sends)
            copy = rdma(
                block(self.buf, src),
                block(self.buf, src),
                ag_send.at[self.phase, k],
                ag_recv.at[self.phase, src],
                target,
            )
            copy.start()
            self.sends.append(copy)

        def arrived(self, src):
            rdma(
                block(self.buf, src),
                block(self.buf, src),
                ag_send.at[self.phase, 0],
                ag_recv.at[self.phase, src],
                index_of(z, y, 1 - c),
            ).wait_recv()

        def spread(self, src):
            self.push(src, index_of(z, 1 - y, c))
            self.push(src, index_of(z_pair, y, c))
            self.push(src, index_of(z, y, 1 - c))

        def begin(self):
            self.push(me, mirror)
            self.spread(me)

        def from_y(self, zz, shift):
            src = (index_of(zz, 1 - y, c) + shift) % n
            self.arrived(src)
            self.push(src, index_of(z, y, 1 - c))

        def from_z(self, shift):
            src = (index_of(z_pair, y, c) + shift) % n
            self.arrived(src)
            self.push(src, index_of(z, 1 - y, c))
            self.push(src, index_of(z, y, 1 - c))

        def pass_on(self, shift):
            self.from_z(shift)
            self.from_y(z, shift)
            if shift == 0:
                self.arrived(mirror)
                self.spread(mirror)

        def settle(self, shift):
            self.from_y(z_pair, shift)
            for zz in (z, z_pair):
                for yy in (y, 1 - y):
                    self.arrived((index_of(zz, yy, 1 - c) + shift) % n)

        def ready(self, shift):
            self.pass_on(shift)
            self.settle(shift)

        def finish(self):
            for copy in self.sends:
                copy.wait_send()

    def scatter(src, dst, phase, group, is_near):
        first = 1 if is_near else 0
        for i in range(first, half):
            p = group * half + (me + i) % half
            rdma(
                block(src, p),
                block(dst, me),
                a2a_send.at[phase, p],
                a2a_recv.at[phase, me],
                p,
            ).start()
        if is_near:
            block(dst, me)[...] = block(src, me)[...]

    def scatter_wait(src, dst, phase, rows=ROWS):
        for i in range(1, n):
            p = (me + i) % n
            rdma(
                block(src, p, rows),
                block(dst, p, rows),
                a2a_send.at[phase, p],
                a2a_recv.at[phase, p],
                p,
            ).wait_recv()

    def scatter_sent(src, dst, phase):
        for i in range(1, n):
            p = (me + i) % n
            rdma(
                block(src, p),
                block(dst, p),
                a2a_send.at[phase, p],
                a2a_recv.at[phase, p],
                p,
            ).wait_send()

    def w_copy(p, landing):
        return rdma(
            w_output.at[:, pl.ds(pl.multiple_of(p * 128, 128), 128)],
            block(w_cols, landing, 128),
            a2a_send.at[3, p],
            a2a_recv.at[3, landing],
            p,
        )

    block(gather_q, me)[...] = norm_rows(states[...], attn_gain[...]).astype(jnp.bfloat16)
    pl.semaphore_wait(barrier, n - 1)

    first = Gather(gather_q, 0)
    first.begin()
    row_id = lax.broadcasted_iota(jnp.int32, (ROWS, 128), 0)
    lane_id = lax.broadcasted_iota(jnp.int32, (ROWS, 128), 1)
    chosen = jnp.concatenate([routes[:, 0, :], routes[:, 1, :]], axis=0)
    shares = jnp.concatenate([gate_weights[0], gate_weights[1]], axis=0)
    weighed = jnp.zeros((ROWS, 128), jnp.float32)
    for k in range(TOPK):
        weighed = jnp.where(lane_id == chosen[:, k : k + 1], shares[:, k : k + 1], weighed)
    gates[...] = weighed
    gates_copy = rdma(gates, mirror_gates, a2a_send.at[5, 1], a2a_recv.at[5, 1], mirror)
    gates_copy.start()
    slot_of = jnp.zeros((ROWS, 128), jnp.int32)
    for b in range(8):
        slot_of = jnp.where(row_id % 8 == b, slots[b], slot_of)
    limits = [jnp.where(slot_of == p, lengths[p], 0) for p in range(2)]
    phases = (limits[0] + limits[1] + row_id // 8).astype(jnp.float32) * rates[...]
    cosine = jnp.cos(phases)
    sine = jnp.sin(phases)
    sine = jnp.where(lane_id < 64, -sine, sine)

    def group_rows(group):
        return pl.ds(pl.multiple_of(group * 128, 128), 128)

    first.ready(0)
    for i in (5, 6, 7):
        loads[i].wait()

    def project(group):
        inputs = gather_q[group_rows(group), :]
        q = jnp.dot(inputs, w_query_v[...], preferred_element_type=jnp.float32)
        kv = lax.dot_general(
            inputs, w_kv_v[...], (((1,), (1,)), ((), ())), preferred_element_type=jnp.float32
        )
        kv = kv.reshape(half, ROWS, 32)
        kv = jnp.concatenate([kv[:, 4 * a : 4 * a + 4, :] for a in range(4)], axis=-1)
        parts[pl.ds(group * half, half), 0:ROWS, :] = q.reshape(half, ROWS, 128)
        parts[pl.ds(group * half, half), ROWS : ROWS + 4, :] = kv
        parts[pl.ds(group * half, half), ROWS + 4 : ROWS + 8, :] = jnp.zeros_like(kv)

    project(near)
    scatter(parts, own_parts, 0, near, True)
    for i in range(half):
        w_copy((1 - near) * half + (me + i) % half, me).start()
    first.ready(half)
    project(1 - near)
    scatter(parts, own_parts, 0, 1 - near, False)
    for i in range(1, half):
        w_copy(near * half + (me + i) % half, me).start()
    first.finish()
    scatter_wait(parts, own_parts, 0)

    def turned(vectors):
        return vectors * cosine + pltpu.roll(vectors, 64, 1) * sine

    for j in range(n):
        rows = slice(j * ROWS, (j + 1) * ROWS)
        queries[rows, :] = turned(own_parts[j, 0:ROWS, :]).astype(jnp.bfloat16)
        packed = own_parts[j, ROWS : ROWS + 4, :]
        unpacked = jnp.concatenate([packed[:, 32 * a : 32 * a + 32] for a in range(4)], axis=0)
        fresh_k[:, j * 16 : (j + 1) * 16] = unpacked[:, 0:16]
        fresh_v[:, j * 16 : (j + 1) * 16] = unpacked[:, 16:32]
    loads[0].wait()
    loads[1].wait()
    inv_root = 1.0 / math.sqrt(HD)
    group_size = HQ // KVH
    q_rows = group_size * ROWS
    span = keys_v.shape[1]
    far_pos = lax.broadcasted_iota(jnp.int32, (q_rows, span), 1)
    row_at = lax.broadcasted_iota(jnp.int32, (q_rows, ROWS), 0) % ROWS
    col_at = lax.broadcasted_iota(jnp.int32, (q_rows, ROWS), 1)
    own_seen = (row_at % 8 == col_at % 8) & (col_at // 8 <= row_at // 8)
    limits = [jnp.concatenate([m[:, 0:1]] * group_size, axis=0) for m in limits]
    for k in range(KVH):
        lanes = slice(k * HD, (k + 1) * HD)
        new_keys = turned(fresh_k[:, lanes]).astype(jnp.bfloat16)
        new_values = fresh_v[:, lanes].astype(jnp.bfloat16)
        appended[:, lanes] = new_keys
        appended[:, slice((KVH + k) * HD, (KVH + k + 1) * HD)] = new_values
        q = queries[k * q_rows : (k + 1) * q_rows, :]

        def against(rows):
            return (
                lax.dot_general(
                    q, rows, (((1,), (1,)), ((), ())), preferred_element_type=jnp.float32
                )
                * inv_root
            )

        scores = [
            jnp.where(far_pos < limits[p], against(keys_v[p, :, lanes]), -1e30) for p in range(2)
        ]
        own_scores = jnp.where(own_seen, against(new_keys), -1e30)
        peak = jnp.maximum(
            jnp.maximum(
                jnp.max(scores[0], axis=1, keepdims=True), jnp.max(scores[1], axis=1, keepdims=True)
            ),
            jnp.max(own_scores, axis=1, keepdims=True),
        )
        weights = [jnp.exp(s - peak) for s in scores]
        own_weights = jnp.exp(own_scores - peak)
        total = (
            jnp.sum(weights[0], axis=1, keepdims=True)
            + jnp.sum(weights[1], axis=1, keepdims=True)
            + jnp.sum(own_weights, axis=1, keepdims=True)
        )
        scale = 1.0 / total
        attended = jnp.dot(
            (own_weights * scale).astype(jnp.bfloat16),
            new_values,
            preferred_element_type=jnp.float32,
        )
        for p in range(2):
            attended = attended + jnp.dot(
                (weights[p] * scale).astype(jnp.bfloat16),
                values_v[p, :, lanes],
                preferred_element_type=jnp.float32,
            )
        attended = attended.astype(jnp.bfloat16)
        for g in range(group_size):
            h = k * group_size + g
            gather_o[pl.ds(pl.multiple_of(me * ROWS, ROWS), ROWS), h * HD : (h + 1) * HD] = (
                attended[g * ROWS : (g + 1) * ROWS, :]
            )

    second = Gather(gather_o, 1)
    second.begin()
    scatter_sent(parts, own_parts, 0)
    loads[4].wait()
    for i in range(1, n):
        w_copy((me + i) % n, (me + i) % n).wait_recv()
    second.ready(0)
    cols[group_rows(near), :] = jnp.dot(
        gather_o[group_rows(near), :], w_cols[...], preferred_element_type=jnp.float32
    )
    scatter(cols, own_cols, 1, near, True)
    second.ready(half)
    cols[group_rows(1 - near), :] = jnp.dot(
        gather_o[group_rows(1 - near), :], w_cols[...], preferred_element_type=jnp.float32
    )
    scatter(cols, own_cols, 1, 1 - near, False)
    second.finish()
    for i in range(1, n):
        w_copy((me + i) % n, (me + i) % n).wait_send()
    scatter_wait(cols, own_cols, 1)
    for j in range(n):
        lanes = slice(j * 128, (j + 1) * 128)
        hidden[:, lanes] = states[:, lanes] + own_cols[j * ROWS : (j + 1) * ROWS, :]
    block(gather_m, me)[...] = norm_rows(hidden[...], moe_gain[...]).astype(jnp.bfloat16)

    third = Gather(gather_m, 2)
    third.begin()
    scatter_sent(cols, own_cols, 1)
    loads[2].wait()
    loads[3].wait()
    ff = down_v.shape[0]

    def gate_up(group):
        @pl.loop(0, ff // 256)
        def _(t):
            at = pl.multiple_of(t * 256, 256)
            inputs = gather_m[group_rows(group), :]
            g = jnp.dot(
                inputs, gate_up_v[:, pl.ds(at, 256)], preferred_element_type=jnp.float32
            )
            u = jnp.dot(
                inputs,
                gate_up_v[:, pl.ds(pl.multiple_of(ff + t * 256, 256), 256)],
                preferred_element_type=jnp.float32,
            )
            act[:, pl.ds(at, 256)] = (g / (1.0 + jnp.exp(-g)) * u).astype(jnp.bfloat16)

    def down(group, part):
        tiles = down_v.shape[1] // 1024

        @pl.loop(part * tiles, (part + 1) * tiles)
        def _(t):
            at = pl.multiple_of(t * 512, 512)
            expert_out[group_rows(group), pl.ds(at, 512)] = jnp.dot(
                act[...], down_v[:, pl.ds(at, 512)], preferred_element_type=jnp.float32
            ).astype(jnp.bfloat16)

    third.ready(0)
    gate_up(near)
    third.pass_on(half)
    down(near, 0)
    down(near, 1)
    third.settle(half)
    gate_up(1 - near)
    wide = down_v.shape[1] // 2

    def strip(ref, i, part):
        rows = pl.ds(pl.multiple_of(i * ROWS, ROWS), ROWS)
        return ref.at[rows, part * wide : (part + 1) * wide]

    def relayed(part, mate, landing):
        return rdma(
            strip(expert_out, (mate + half) % n, part),
            strip(relay, landing % half, part),
            a2a_send.at[4 + 2 * part, mate],
            a2a_recv.at[4 + 2 * part, landing],
            mate,
        )

    for part in range(2):
        down(1 - near, part)
        for i in range(1, half):
            relayed(part, near * half + (me + i) % half, me).start()
    for i in range(1, half):
        mate = near * half + (me + i) % half
        rdma(
            block(expert_out, mate),
            block(returned, me % half),
            a2a_send.at[2, mate],
            a2a_recv.at[2, me],
            mate,
        ).start()
    third.finish()

    def mixed(total, shares, e, got):
        share = jnp.sum(jnp.where(lane_id == e, shares[...], 0.0), axis=1, keepdims=True)
        return total + jnp.where(share > 0.0, share * got[...].astype(jnp.float32), 0.0)

    gates_copy.wait()
    sums = []
    for part in range(2):
        total = mixed(
            jnp.zeros((ROWS, wide), jnp.float32), mirror_gates, me, strip(expert_out, mirror, part)
        )
        for i in range(1, half):
            e = near * half + (me + i) % half
            relayed(part, e, e).wait_recv()
            total = mixed(total, mirror_gates, e, strip(relay, e % half, part))
        strip(summed, 0, part)[...] = total
        copy = rdma(
            strip(summed, 0, part),
            strip(from_mirror, 0, part),
            a2a_send.at[5, 2 + part],
            a2a_recv.at[5, 2 + part],
            mirror,
        )
        copy.start()
        sums.append(copy)

    def back(e):
        return rdma(
            block(expert_out, e),
            block(returned, e % half),
            a2a_send.at[2, e],
            a2a_recv.at[2, e],
            e,
        )

    total = mixed(hidden[...], gates, me, block(expert_out, me))
    for i in range(1, half):
        e = near * half + (me + i) % half
        back(e).wait_recv()
        total = mixed(total, gates, e, block(returned, e % half))
    for copy in sums:
        copy.wait()
    out[...] = total + from_mirror[...]
    for i in range(1, half):
        e = near * half + (me + i) % half
        back(e).wait_send()
        for part in range(2):
            relayed(part, e, e).wait_send()


def tuned(
    states,
    attn_gain,
    moe_gain,
    w_query,
    w_key,
    w_value,
    w_output,
    w_gate_up,
    w_down,
    key_cache,
    value_cache,
    cache_lengths,
    prefix_slot,
    routes,
    gate_weights,
):
    n = lax.axis_size("ep")
    step_count, row_count, width = states.shape
    rows = step_count * row_count
    prefix_count, span, kv_width = key_cache.shape
    ff = w_down.shape[1]
    inverse_rate = THETA ** (-(jnp.arange(HD // 2).astype(jnp.float32) * 2.0 / HD))
    rates = jnp.tile(inverse_rate, 2).reshape(1, HD)
    in_vmem = pl.BlockSpec(memory_space=pltpu.VMEM)
    in_smem = pl.BlockSpec(memory_space=pltpu.SMEM)
    in_hbm = pl.BlockSpec(memory_space=pl.ANY)
    everyone = n * rows
    bf16, f32 = jnp.bfloat16, jnp.float32
    out, appended = pl.pallas_call(
        layer_kernel,
        out_shape=(
            jax.ShapeDtypeStruct((rows, width), f32),
            jax.ShapeDtypeStruct((rows, 2 * kv_width), bf16),
        ),
        in_specs=[in_vmem] * 4 + [in_smem] * 2 + [in_vmem] * 2 + [in_hbm] * 8,
        out_specs=(in_vmem, in_vmem),
        scratch_shapes=[
            pltpu.VMEM((width, 128), bf16),
            pltpu.VMEM((32, width), bf16),
            pltpu.VMEM((rows, 128), f32),
            pltpu.VMEM((rows, 128), f32),
            pltpu.VMEM((everyone // 2, width), bf16),
            pltpu.VMEM((rows, width), f32),
            pltpu.VMEM((rows, width), f32),
            pltpu.VMEM((everyone, width), bf16),
            pltpu.VMEM((everyone, width), bf16),
            pltpu.VMEM((everyone, width), bf16),
            pltpu.VMEM((n, rows + 8, 128), f32),
            pltpu.VMEM((n, rows + 8, 128), f32),
            pltpu.VMEM((width, 128), bf16),
            pltpu.VMEM((everyone, 128), f32),
            pltpu.VMEM((everyone, 128), f32),
            pltpu.VMEM((rows, width), f32),
            pltpu.VMEM((everyone // 2, ff), bf16),
            pltpu.VMEM((everyone, width), bf16),
            pltpu.VMEM((everyone // 2, width), bf16),
            pltpu.VMEM((rows, kv_width), f32),
            pltpu.VMEM((rows, kv_width), f32),
            pltpu.VMEM((HQ * rows, HD), bf16),
            pltpu.VMEM((width, 2 * ff), bf16),
            pltpu.VMEM((ff, width), bf16),
            pltpu.VMEM((prefix_count, span, kv_width), bf16),
            pltpu.VMEM((prefix_count, span, kv_width), bf16),
            pltpu.SemaphoreType.DMA((8,)),
            pltpu.SemaphoreType.DMA((3, 16)),
            pltpu.SemaphoreType.DMA((3, 16)),
            pltpu.SemaphoreType.DMA((7, 16)),
            pltpu.SemaphoreType.DMA((7, 16)),
        ],
        compiler_params=pltpu.CompilerParams(
            collective_id=0, has_side_effects=True, vmem_limit_bytes=56 * 1024 * 1024
        ),
    )(
        states.reshape(rows, width),
        attn_gain.reshape(1, width),
        moe_gain.reshape(1, width),
        rates,
        cache_lengths,
        prefix_slot,
        routes,
        gate_weights,
        w_query,
        w_key.T,
        w_value.T,
        w_output,
        w_gate_up[0],
        w_down[0],
        key_cache,
        value_cache,
    )
    return (
        out.reshape(step_count, row_count, width),
        appended.reshape(step_count, row_count, 2 * kv_width),
    )


def solution(mesh):
    return jax.shard_map(
        tuned if mesh.shape["ep"] == TUNED_DEVICES else shards,
        mesh=mesh,
        in_specs=(
            P(None, ("groups", "ep"), None),
            P(),
            P(),
            P(None, "ep"),
            P(None, "ep"),
            P(None, "ep"),
            P("ep", None),
            P("ep", None, None),
            P("ep", None, None),
            P(("groups", "ep"), None, None),
            P(("groups", "ep"), None, None),
            P(("groups", "ep")),
            P(("groups", "ep")),
            P(("groups", "ep"), None, None),
            P(None, ("groups", "ep"), None),
        ),
        out_specs=(P(None, ("groups", "ep"), None), P(None, ("groups", "ep"), None)),
        check_vma=False,
    )
```
